256 devices in a mesh: dom: 256 (over y, x, z, core).
Axes of the slice: x: 4, y: 4, z: 8, core: 2. Of those that a mesh axis runs over, the one named last changes fastest.
Arguments:
- rhs: float32 [8, 1703936], P(None, 'dom'), may hold values from -25 to 25, as said below
- potential: float32 [1703936], P('dom'), may hold values from 0.5 to 2
- precond: float32 [1703936], P('dom'), may hold values from 0.05 to 0.5
- shift: float32 [8], replicated, may hold values from 0.3 to 3
- stiffness: float32 [343, 343], replicated, may hold values from -0.4 to 2, as said below
- cell_scale: float32 [8192], P('dom'), may hold values from 0.5 to 2
- conn: int32 [8192, 343], P('dom'), may hold values from 0 to 7487, as said below
- cell_count: int32 [256], replicated, may hold values from 1 to 32, as said below
- projector: float32 [2048, 8, 343], P('dom'), may hold values from -0.6 to 0.6
- support_cell: int32 [2048], P('dom'), may hold values from 0 to 31, as said below
- support_atom: int32 [2048], P('dom'), may hold values from 0 to 511, as said below
- support_count: int32 [256], replicated, may hold values from 4 to 8, as said below
- atom_matrix: float32 [512, 8, 8], P('dom'), may hold values from -2 to 15, as said below
Outputs:
- solution: float32 [8, 1703936], P(None, 'dom')
- residual: float32 [8, 1703936], P(None, 'dom')
The draws below stay inside these ranges and needn't reach their ends.
Inputs may be any that keep to these rules, and one draw needn't show every extreme that they name: `rhs`: row v rises in scale along the nodes. `stiffness`: symmetric positive definite. `atom_matrix`: each atom's matrix is symmetric positive definite. Block b's live cells are its slots 0 to cell_count[b] - 1; blocks 2k and 2k + 1 together hold at most 40 live cells, and some block holds 32. `conn`: a local index i of block b is column b * 6656 + i of the field padded by 416 zero columns at each end: indices below 416 are the previous block's last nodes, indices from 7072 on the next block's first nodes. `support_cell`: every entry names a live cell of its block. `support_atom`: atom a is owned by block a // 2; an entry of block b names an atom owned by block b - 1, b or b + 1. Block b's live entries are its first support_count[b]; some block has 8.
All inputs are finite; a program needn't handle non-finite values.
Results may differ from the reference program's by a relative error of at most 0.0003.
Values sent between devices are 32-bit elements; how exact they have to be, the bound alone decides.
A program may use at most 64 MiB of HBM per device.

```python
import math
import jax
import jax.numpy as jnp
from jax import lax

ELEM = 343
NPROJ = 8
VEC = 8
ITERS = 2
CELL_DEV = 32
NODE_DEV = 6656
GHOST = 416
HALF = 20
PSUP_DEV = 8
ATOM_DEV = 2
NODES = 1703936
CELLS = 8192
PSUPS = 2048
ATOMS = 512
N_DOM = 256


def pair_counts(key):
    pairs = N_DOM // 2
    keys = jax.random.split(key, 4)
    totals = jax.random.randint(keys[0], (pairs,), HALF, 2 * HALF + 1)
    upper = jnp.minimum(totals - 1, CELL_DEV)
    lower = (totals + 1) // 2
    heavy = jax.random.randint(keys[1], (pairs,), lower, upper + 1)
    chosen = jax.random.randint(keys[2], (), 0, pairs)
    marked = jnp.arange(pairs) == chosen
    totals = jnp.where(marked, 2 * HALF, totals)
    heavy = jnp.where(marked, CELL_DEV, heavy)
    light = totals - heavy
    first = jax.random.randint(keys[3], (pairs,), 0, 2)
    even = jnp.where(first == 1, heavy, light)
    odd = jnp.where(first == 1, light, heavy)
    return jnp.stack([even, odd], axis=1).reshape(N_DOM).astype(jnp.int32)


def draw_cell_count(key, part):
    return pair_counts(jax.random.fold_in(key, 7))


def draw_support_cell(key, part):
    counts = pair_counts(jax.random.fold_in(key, 7))
    owner = jnp.arange(PSUPS) // PSUP_DEV
    return jax.random.randint(jax.random.fold_in(key, 13), (PSUPS,), 0, counts[owner]).astype(jnp.int32)


def draw_support_atom(key, part):
    keys = jax.random.split(jax.random.fold_in(key, 17), 2)
    block = jnp.arange(PSUPS) // PSUP_DEV
    offset = jax.random.randint(keys[0], (PSUPS,), -1, 2)
    owner = jnp.clip(block + offset, 0, N_DOM - 1)
    local = jax.random.randint(keys[1], (PSUPS,), 0, ATOM_DEV)
    return (owner * ATOM_DEV + local).astype(jnp.int32)


def draw_support_count(key, part):
    keys = jax.random.split(jax.random.fold_in(key, 19), 2)
    counts = jax.random.randint(keys[0], (N_DOM,), PSUP_DEV // 2, PSUP_DEV + 1)
    chosen = jax.random.randint(keys[1], (), 0, N_DOM)
    return jnp.where(jnp.arange(N_DOM) == chosen, PSUP_DEV, counts).astype(jnp.int32)


def draw_conn(key, part):
    keys = jax.random.split(jax.random.fold_in(key, 23), 4)
    reach = NODE_DEV // 4
    base = jax.random.randint(keys[0], (CELLS, 1), 0, NODE_DEV + 2 * GHOST - reach + 1)
    spread = jax.random.randint(keys[1], (CELLS, ELEM), 0, reach)
    nodes = base + spread
    low_rim = jax.random.randint(keys[2], (CELLS,), 0, GHOST)
    high_rim = jax.random.randint(keys[3], (CELLS,), GHOST + NODE_DEV, NODE_DEV + 2 * GHOST)
    nodes = nodes.at[:, 0].set(low_rim)
    nodes = nodes.at[:, ELEM - 1].set(high_rim)
    return nodes.astype(jnp.int32)


def draw_rhs(key, part):
    keys = jax.random.split(jax.random.fold_in(key, 29), 1)
    ramp = 1.0 + 2.0 * jnp.arange(NODES, dtype=jnp.float32) / NODES
    rough = jax.random.truncated_normal(keys[0], -4.0, 4.0, (VEC, NODES), jnp.float32)
    return (rough * ramp[None, :]).astype(jnp.float32)


def draw_stiffness(key, part):
    inner = jax.random.fold_in(key, 31)
    raw = jnp.clip(jax.random.normal(inner, (ELEM, ELEM), jnp.float32), -4.0, 4.0)
    sym = 0.5 * (raw + raw.T)
    outside = sym * (1.0 - jnp.eye(ELEM, dtype=jnp.float32))
    diagonal = 1.0 + jnp.sum(jnp.abs(outside), axis=1)
    matrix = outside + jnp.diag(diagonal)
    return (matrix / jnp.mean(diagonal)).astype(jnp.float32)


def draw_atom_matrix(key, part):
    inner = jax.random.fold_in(key, 37)
    raw = 0.5 * jnp.clip(jax.random.normal(inner, (ATOMS, NPROJ, NPROJ), jnp.float32), -4.0, 4.0)
    sym = 0.5 * (raw + jnp.swapaxes(raw, 1, 2))
    outside = sym * (1.0 - jnp.eye(NPROJ, dtype=jnp.float32))[None, :, :]
    diagonal = 0.5 + jnp.sum(jnp.abs(outside), axis=2)
    matrix = outside + diagonal[:, :, None] * jnp.eye(NPROJ, dtype=jnp.float32)[None, :, :]
    return matrix.astype(jnp.float32)


def shard_levels(stream_key, shape, pieces, least, top_value):
    level, own = 1.0, jax.random.fold_in(stream_key, 6)
    for dim, parts in pieces:
        draws = jnp.exp(jax.random.uniform(jax.random.fold_in(own, dim), (parts,), jnp.float32, least / len(pieces), top_value / len(pieces)))
        level = level * jnp.repeat(draws, shape[dim] // parts).reshape([-1 if axis == dim else 1 for axis in range(len(shape))])
    return level


def bell_draw(key, shape, deviation, limit, cuts=(), held_as=jnp.bfloat16):
    result = jax.random.normal(key, shape, jnp.float32) * deviation
    if len(cuts) > 0:
        result = shard_levels(key, shape, cuts, -0.22, 0.18) * result
    return jnp.clip(result, min=-limit, max=limit).astype(held_as)


def setup_inputs(seed: int = 0) -> dict:
    streams_of = jax.random.split(jax.random.key(seed), 14)
    return {
        "rhs": draw_rhs(jax.random.fold_in(streams_of[13], 71), 0),
        "potential": jnp.clip(0.5 + 1.5 * jax.random.uniform(streams_of[1], (NODES,), jnp.float32) ** shard_levels(streams_of[1], (NODES,), ((0, 256),), -0.2, 0.2), 0.5, 2.0),
        "precond": jnp.clip(jnp.exp(math.log(0.5) - 2.3025851 * jax.random.uniform(streams_of[2], (NODES,), jnp.float32) ** shard_levels(streams_of[2], (NODES,), ((0, 256),), -0.2, 0.2)), 0.05, 0.5),
        "shift": jnp.clip(jnp.exp(jax.random.uniform(streams_of[3], (VEC,), jnp.float32, math.log(0.3), math.log(3.0))), 0.3, 3.0),
        "stiffness": draw_stiffness(jax.random.fold_in(streams_of[13], 71), 0),
        "cell_scale": jnp.clip(jnp.exp(math.log(2.0) - 1.3862944 * jax.random.uniform(streams_of[5], (CELLS,), jnp.float32) ** shard_levels(streams_of[5], (CELLS,), ((0, 256),), -0.2, 0.2)), 0.5, 2.0),
        "conn": draw_conn(jax.random.fold_in(streams_of[13], 71), 0),
        "cell_count": draw_cell_count(jax.random.fold_in(streams_of[13], 71), 0),
        "projector": bell_draw(streams_of[8], (PSUPS, NPROJ, ELEM), 0.1, 0.6, ((0, 256),), jnp.float32),
        "support_cell": draw_support_cell(jax.random.fold_in(streams_of[13], 71), 0),
        "support_atom": draw_support_atom(jax.random.fold_in(streams_of[13], 71), 0),
        "support_count": draw_support_count(jax.random.fold_in(streams_of[13], 71), 0),
        "atom_matrix": draw_atom_matrix(jax.random.fold_in(streams_of[13], 71), 0),
    }


HIGH = lax.Precision.HIGHEST


def apply_operator(field, potential, shift, stiffness, cell_scale, conn, cell_count, projector, support_cell, support_atom, support_count, atom_matrix):
    padded = jnp.pad(field, ((0, 0), (GHOST, GHOST)))
    conn_blocks = conn.reshape(N_DOM, CELL_DEV, ELEM)
    scale_blocks = cell_scale.reshape(N_DOM, CELL_DEV)
    proj_blocks = projector.reshape(N_DOM, PSUP_DEV, NPROJ, ELEM)
    cell_blocks = support_cell.reshape(N_DOM, PSUP_DEV)
    blocks = jnp.arange(N_DOM, dtype=jnp.int32)
    entry_live = (jnp.arange(PSUP_DEV, dtype=jnp.int32)[None, :] < support_count[:, None]).astype(field.dtype)

    def window_of(index):
        return lax.dynamic_slice_in_dim(padded, (index * NODE_DEV).astype(jnp.int32), NODE_DEV + 2 * GHOST, 1)

    def partials(index):
        window = window_of(index)
        rows = conn_blocks[index][cell_blocks[index]]
        values = window[:, rows]
        return jnp.einsum("sjn,vsn->sjv", proj_blocks[index], values, precision=HIGH)

    weights = lax.map(partials, blocks)
    weights = weights * entry_live[:, :, None, None]
    flat = weights.reshape(N_DOM * PSUP_DEV, NPROJ, VEC)
    coef = jax.ops.segment_sum(flat, support_atom, num_segments=ATOMS)
    term = jnp.einsum("aij,ajv->aiv", atom_matrix, coef, precision=HIGH)
    picked = term[support_atom] * entry_live.reshape(-1)[:, None, None]
    picked = picked.reshape(N_DOM, PSUP_DEV, NPROJ, VEC)

    def local(index):
        window = window_of(index)
        connect = conn_blocks[index]
        live = (jnp.arange(CELL_DEV, dtype=jnp.int32) < cell_count[index]).astype(field.dtype)
        values = window[:, connect] * (scale_blocks[index] * live)[None, :, None]
        product = jnp.einsum("vcn,mn->vcm", values, stiffness, precision=HIGH)
        rows = connect[cell_blocks[index]]
        back = jnp.einsum("sjn,sjv->vsn", proj_blocks[index], picked[index], precision=HIGH)
        total = jnp.zeros_like(window)
        total = total.at[:, connect].add(product)
        total = total.at[:, rows].add(back)
        return total

    stacked = lax.map(local, blocks)
    inner = jnp.transpose(stacked[:, :, GHOST:GHOST + NODE_DEV], (1, 0, 2))
    left = jnp.transpose(stacked[:, :, :GHOST], (1, 0, 2))
    right = jnp.transpose(stacked[:, :, GHOST + NODE_DEV:], (1, 0, 2))
    inner = inner.at[:, :-1, NODE_DEV - GHOST:].add(left[:, 1:])
    inner = inner.at[:, 1:, :GHOST].add(right[:, :-1])
    return inner.reshape(VEC, NODES) + (potential[None, :] + shift[:, None]) * field


def reference(rhs, potential, precond, shift, stiffness, cell_scale, conn, cell_count, projector, support_cell, support_atom, support_count, atom_matrix):
    def operator(field):
        return apply_operator(field, potential, shift, stiffness, cell_scale, conn, cell_count, projector, support_cell, support_atom, support_count, atom_matrix)

    solution = jnp.zeros_like(rhs)
    residual = rhs
    search = precond[None, :] * residual
    gamma = jnp.sum(residual * search, axis=1)
    for step in range(ITERS):
        image = operator(search)
        step_size = gamma / jnp.sum(search * image, axis=1)
        solution = solution + step_size[:, None] * search
        residual = residual - step_size[:, None] * image
        if step + 1 < ITERS:
            smoothed = precond[None, :] * residual
            fresh = jnp.sum(residual * smoothed, axis=1)
            search = smoothed + (fresh / gamma)[:, None] * search
            gamma = fresh
    return solution, residual
```

```python
import jax
import jax.numpy as jnp
from jax import lax
from jax.experimental import pallas as pl
from jax.experimental.pallas import tpu as pltpu
from jax.sharding import PartitionSpec as P

F32 = jnp.float32
BF16 = jnp.bfloat16
HIGH = lax.Precision.HIGHEST
MESH = pl.DeviceIdType.MESH

VEC = 8
NPROJ = 8
ELEM = 343
PAD = 384
CELLS = 32
PAIRS = CELLS // 2
ENTRIES = 8
OWNED = 2
NODE_DEV = 6656
GHOST = 416
LANES = 256
OWN = NODE_DEV // LANES
EDGE = 2
ROWS = OWN + 2 * EDGE
SHIFT = EDGE * LANES - GHOST
N_DOM = 256


def kernel(
    count_ref,
    support_cell_ref,
    support_atom_ref,
    support_count_ref,
    shift_ref,
    scale_ref,
    rhs_ref,
    pot_ref,
    pre_ref,
    stiff_ref,
    conn_ref,
    proj_ref,
    atom_ref,
    sol_ref,
    res_ref,
    win,
    win_split,
    onehot,
    hi_ref,
    values,
    lhs_hi,
    lhs_lo,
    stiff_hi,
    stiff_lo,
    proj_pad,
    spread_ref,
    product,
    packed,
    acc,
    v_one,
    v_two,
    rim_left,
    rim_right,
    pre_out,
    pre_in,
    atom_in,
    coef_out,
    coef_m2,
    coef_m1,
    coef_p1,
    coef_p2,
    red_out,
    red_in,
    send_sem,
    recv_sem,
):
    me = lax.axis_index("dom")

    def ring(step):
        return lax.rem(me + (step + N_DOM), N_DOM)

    z = lax.rem(lax.div(me, 2), 8)
    x_core = lax.rem(lax.div(me, 16), 4) * 2 + lax.rem(me, 2)
    y = lax.div(me, 64)
    base_z = me - 2 * z
    base_xc = me - 16 * lax.rem(lax.div(me, 16), 4) - lax.rem(me, 2)
    base_y = me - 64 * y

    def z_partner(d):
        return base_z + 2 * lax.rem(z + d, 8)

    def xc_partner(d):
        other = lax.rem(x_core + d, 8)
        return base_xc + 16 * lax.div(other, 2) + lax.rem(other, 2)

    def y_partner(d):
        return base_y + 64 * lax.rem(y + d, 4)

    stages = (
        [z_partner(d) for d in range(1, 8)],
        [xc_partner(d) for d in range(1, 8)],
        [y_partner(d) for d in range(1, 4)],
    )
    greeted = [ring(-2), ring(-1), ring(1), ring(2)]
    for group in stages:
        greeted = greeted + group
    barrier = pltpu.get_barrier_semaphore()
    for other in greeted:
        pl.semaphore_signal(barrier, inc=1, device_id=(other,), device_id_type=MESH)

    used = [0]

    def send(src, dst, target):
        slot = used[0]
        used[0] = slot + 1
        copy = pltpu.make_async_remote_copy(
            src_ref=src,
            dst_ref=dst,
            send_sem=send_sem.at[slot],
            recv_sem=recv_sem.at[slot],
            device_id=(target,),
            device_id_type=MESH,
        )
        copy.start()
        return copy

    def row(ref, index):
        return jnp.broadcast_to(ref[index : index + 1, :], (VEC, 128))

    dot_acc = jnp.zeros((VEC, 128), F32)
    for k in range(OWN):
        for t in range(2):
            column = LANES * k + 128 * t
            r = rhs_ref[:, column : column + 128]
            p = r * row(pre_ref, 2 * k + t)
            win[EDGE + k, :, 128 * t : 128 * t + 128] = p
            dot_acc = dot_acc + r * p
    gamma = jnp.sum(dot_acc, axis=1, keepdims=True)
    pre_out[...] = jnp.zeros_like(pre_out)
    pre_out[0, 0:4, :] = pre_ref[0:4, :]
    pre_out[1, 0:4, :] = pre_ref[48:52, :]

    pl.semaphore_wait(barrier, len(greeted))
    first = [
        send(win.at[EDGE : 2 * EDGE], win.at[ROWS - EDGE : ROWS], ring(-1)),
        send(win.at[OWN : OWN + EDGE], win.at[0:EDGE], ring(1)),
        send(pre_out.at[0], pre_in.at[1], ring(-1)),
        send(pre_out.at[1], pre_in.at[0], ring(1)),
        send(atom_ref, atom_in.at[1], ring(-1)),
        send(atom_ref, atom_in.at[0], ring(1)),
    ]

    position = jnp.full((CELLS, PAD), -1, jnp.int32)
    lane = lax.broadcasted_iota(jnp.int32, (1, PAD), 1)
    spread_ref[...] = position
    spread_ref[:, 0:ELEM] = conn_ref[...] + SHIFT
    for c in range(CELLS):
        hi_ref[c] = spread_ref[c : c + 1, :]

    def build(c, carry):
        number = lax.broadcasted_iota(jnp.int32, (LANES, PAD), 0)
        for q in range(2):
            low = jnp.bitwise_and(hi_ref[2 * c + q], LANES - 1)
            hit = jnp.where(number == low, 1.0, 0.0).astype(BF16)
            onehot[c, :, PAD * q : PAD * q + PAD] = hit
        return carry

    lax.fori_loop(0, PAIRS, build, 0)
    for c in range(CELLS):
        hi_ref[c] = jnp.right_shift(hi_ref[c], 8)
    stiff_hi[...] = jnp.zeros_like(stiff_hi)
    stiff_lo[...] = jnp.zeros_like(stiff_lo)
    stiff = stiff_ref[...]
    top = stiff.astype(BF16)
    stiff_hi[0:ELEM, 0:ELEM] = top
    stiff_lo[0:ELEM, 0:ELEM] = (stiff - top.astype(F32)).astype(BF16)
    proj_pad[...] = jnp.zeros_like(proj_pad)
    proj_pad[:, 0:ELEM] = proj_ref[...]

    lane64 = lax.broadcasted_iota(jnp.int32, (1, 64), 1)
    entry_of = jnp.right_shift(lane64, 3)
    live_entries = support_count_ref[me]
    cell_row = jnp.full((1, 64), -1, jnp.int32)
    atom_row = jnp.full((1, 64), -1, jnp.int32)
    relative = []
    for s in range(ENTRIES):
        live = s < live_entries
        own_atom = jnp.where(live, support_atom_ref[s] - (me - 1) * OWNED, -1)
        relative.append(own_atom)
        cell_row = jnp.where(entry_of == s, support_cell_ref[s], cell_row)
        atom_row = jnp.where(entry_of == s, own_atom, atom_row)
    live_cells = count_ref[me]
    sublane = lax.broadcasted_iota(jnp.int32, (VEC, 128), 0)
    shift_col = jnp.zeros((VEC, 128), F32)
    for v in range(VEC):
        shift_col = jnp.where(sublane == v, shift_ref[v], shift_col)
    r64 = lax.broadcasted_iota(jnp.int32, (64, 48), 0)
    c48 = lax.broadcasted_iota(jnp.int32, (64, 48), 1)
    fold = jnp.where(jnp.bitwise_and(r64, 7) == jnp.bitwise_and(c48, 7), 1.0, 0.0).astype(F32)
    r48 = lax.broadcasted_iota(jnp.int32, (48, 48), 0)
    d48 = lax.broadcasted_iota(jnp.int32, (48, 48), 1)
    same_atom = jnp.right_shift(r48, 3) == jnp.right_shift(d48, 3)
    r8 = lax.broadcasted_iota(jnp.int32, (8, 64), 0)
    c64 = lax.broadcasted_iota(jnp.int32, (8, 64), 1)
    tile8 = jnp.where(r8 == jnp.bitwise_and(c64, 7), 1.0, 0.0).astype(F32)

    for copy in first:
        copy.wait()
    not_first = me > 0
    not_last = me < N_DOM - 1
    for k in range(EDGE):
        win[k] = jnp.where(not_first, win[k], 0.0)
        win[ROWS - EDGE + k] = jnp.where(not_last, win[ROWS - EDGE + k], 0.0)
    atoms = jnp.concatenate([atom_in[0], atom_ref[...], atom_in[1]], axis=0)
    atom_tiled = jnp.dot(atoms, tile8, precision=HIGH, preferred_element_type=F32)

    def gather():
        w = win[...].reshape(ROWS * VEC, LANES)
        wh = w.astype(BF16)
        win_split[:, 0:LANES] = wh
        win_split[:, LANES:] = (w - wh.astype(F32)).astype(BF16)

        def body(c, carry):
            oh = onehot[c]
            g = jnp.dot(win_split[:, 0:LANES], oh, preferred_element_type=F32) + jnp.dot(
                win_split[:, LANES:], oh, preferred_element_type=F32
            )
            his, los = [], []
            for q in range(2):
                cell = 2 * c + q
                weight = jnp.where(cell < live_cells, scale_ref[cell], 0.0)
                parts = []
                for t in range(3):
                    h = jnp.broadcast_to(hi_ref[cell, :, 128 * t : 128 * t + 128], (VEC, 128))
                    got = jnp.zeros((VEC, 128), F32)
                    at = PAD * q + 128 * t
                    for k in range(ROWS):
                        got = jnp.where(h == k, g[VEC * k : VEC * k + VEC, at : at + 128], got)
                    parts.append(got)
                full = jnp.concatenate(parts, axis=1)
                values[cell] = full
                scaled = full * weight
                up = scaled.astype(BF16)
                his.append(up)
                los.append((scaled - up.astype(F32)).astype(BF16))
            lhs_hi[c] = jnp.concatenate(his, axis=0)
            lhs_lo[c] = jnp.concatenate(los, axis=0)
            return carry

        lax.fori_loop(0, PAIRS, body, 0, unroll=2)

    def scatter(first_step, last_step):
        def body(c, carry):
            vs, hs = [], []
            for q in range(2):
                cell = 2 * c + q
                vs.append(packed[cell])
                hs.append(jnp.broadcast_to(hi_ref[cell], (16, PAD)).astype(jnp.int16))
            v = jnp.concatenate(vs, axis=1)
            h = jnp.concatenate(hs, axis=1)
            zero = jnp.zeros_like(v)
            a = jnp.concatenate([jnp.where(h == k, v, zero) for k in range(ROWS)], axis=0)
            acc[...] += lax.dot_general(
                a, onehot[c], (((1,), (1,)), ((), ())), preferred_element_type=F32
            )
            return carry

        lax.fori_loop(first_step, last_step, body, 0, unroll=2)

    def element_work(step):
        picked = jnp.concatenate([values[support_cell_ref[s]] for s in range(ENTRIES)], axis=0)
        cross = lax.dot_general(
            picked,
            proj_pad[...],
            (((1,), (1,)), ((), ())),
            precision=HIGH,
            preferred_element_type=F32,
        )
        own = [jnp.zeros((VEC, 64), F32) for _ in range(3 * OWNED)]
        for s in range(ENTRIES):
            mine = jnp.where(entry_of == s, cross[VEC * s : VEC * s + VEC, :], 0.0)
            for a in range(3 * OWNED):
                own[a] = own[a] + jnp.where(relative[s] == a, mine, 0.0)
        for a in range(3 * OWNED):
            coef_out[step, a, :, 0:64] = own[a]
        coefs = [
            send(coef_out.at[step, 0:4], coef_p1.at[step], ring(-1)),
            send(coef_out.at[step, 2:6], coef_m1.at[step], ring(1)),
            send(coef_out.at[step, 0:2], coef_p2.at[step], ring(-2)),
            send(coef_out.at[step, 4:6], coef_m2.at[step], ring(2)),
        ]
        uh = lhs_hi[...].reshape(CELLS * VEC, PAD)
        ul = lhs_lo[...].reshape(CELLS * VEC, PAD)
        out = jnp.dot(uh, stiff_hi[...], preferred_element_type=F32)
        out = out + jnp.dot(uh, stiff_lo[...], preferred_element_type=F32)
        out = out + jnp.dot(ul, stiff_hi[...], preferred_element_type=F32)
        product[...] = out.reshape(CELLS, VEC, PAD)
        for copy in coefs:
            copy.wait()
        left2, left1 = coef_m2[step], coef_m1[step]
        right1, right2 = coef_p1[step], coef_p2[step]
        total = [
            own[0] + left1[0, :, 0:64] + left2[0, :, 0:64],
            own[1] + left1[1, :, 0:64] + left2[1, :, 0:64],
            own[2] + left1[2, :, 0:64] + right1[0, :, 0:64],
            own[3] + left1[3, :, 0:64] + right1[1, :, 0:64],
            own[4] + right1[2, :, 0:64] + right2[0, :, 0:64],
            own[5] + right1[3, :, 0:64] + right2[1, :, 0:64],
        ]
        stacked = jnp.concatenate(total, axis=0)
        coef = jnp.dot(stacked, fold, precision=HIGH, preferred_element_type=F32)
        coef = jnp.where(same_atom, coef, 0.0)
        term = jnp.dot(coef, atom_tiled, precision=HIGH, preferred_element_type=F32)
        chosen = jnp.zeros((VEC, 64), F32)
        for a in range(3 * OWNED):
            chosen = chosen + jnp.where(atom_row == a, term[VEC * a : VEC * a + VEC, :], 0.0)
        back = jnp.concatenate(
            [jnp.where(cell_row == c, chosen, 0.0) for c in range(CELLS)], axis=0
        )
        support = jnp.dot(back, proj_pad[...], precision=HIGH, preferred_element_type=F32)
        product[...] = product[...] + support.reshape(CELLS, VEC, PAD)

        def pack(c, energy):
            full = product[c]
            up = full.astype(BF16)
            packed[c] = jnp.concatenate([up, (full - up.astype(F32)).astype(BF16)], axis=0)
            return energy + full * values[c]

        return lax.fori_loop(0, CELLS, pack, jnp.zeros((VEC, PAD), F32), unroll=4)

    def diagonal(k, t):
        at = slice(128 * t, 128 * t + 128)
        return (row(pot_ref, 2 * k + t) + shift_col) * win[EDGE + k, :, at]

    gather()
    element_work(0)
    acc[...] = jnp.zeros_like(acc)
    scatter(0, PAIRS)
    for k in range(ROWS):
        both = acc[16 * k : 16 * k + 8, :] + acc[16 * k + 8 : 16 * k + 16, :]
        if EDGE <= k < EDGE + OWN:
            extra = jnp.concatenate([diagonal(k - EDGE, t) for t in range(2)], axis=1)
            both = both + extra
        v_one[k] = both
    rims = [
        send(v_one.at[0 : 2 * EDGE], rim_right.at[0], ring(-1)),
        send(v_one.at[OWN:ROWS], rim_left.at[0], ring(1)),
    ]
    for copy in rims:
        copy.wait()
    for k in range(2 * EDGE):
        v_one[k] = v_one[k] + jnp.where(not_first, rim_left[0, k], 0.0)
        v_one[OWN + k] = v_one[OWN + k] + jnp.where(not_last, rim_right[0, k], 0.0)

    a_acc = jnp.zeros((VEC, 128), F32)
    c_acc = jnp.zeros((VEC, 128), F32)
    d_acc = jnp.zeros((VEC, 128), F32)
    for k in range(OWN):
        for t in range(2):
            at = slice(128 * t, 128 * t + 128)
            image = v_one[EDGE + k, :, at]
            a_acc = a_acc + image * win[EDGE + k, :, at]
            w = image * row(pre_ref, 2 * k + t)
            win[EDGE + k, :, at] = w
            c_acc = c_acc + image * w
            d_acc = d_acc + (row(pot_ref, 2 * k + t) + shift_col) * w * w
    for k in range(EDGE):
        for t in range(2):
            at = slice(128 * t, 128 * t + 128)
            left = row(pre_in.at[0], 2 * k + t) * v_one[k, :, at]
            win[k, :, at] = jnp.where(not_first, left, 0.0)
            right = row(pre_in.at[1], 2 * k + t) * v_one[OWN + EDGE + k, :, at]
            win[OWN + EDGE + k, :, at] = jnp.where(not_last, right, 0.0)

    gather()
    energy = element_work(1)
    for t in range(3):
        d_acc = d_acc + energy[:, 128 * t : 128 * t + 128]
    a_sum = jnp.sum(a_acc, axis=1, keepdims=True)
    c_sum = jnp.sum(c_acc, axis=1, keepdims=True)
    d_sum = jnp.sum(d_acc, axis=1, keepdims=True)
    column = lax.broadcasted_iota(jnp.int32, (VEC, 128), 1)
    tile = jnp.where(
        column == 0,
        gamma,
        jnp.where(column == 1, a_sum, jnp.where(column == 2, c_sum, jnp.where(column == 3, d_sum, 0.0))),
    )

    def reduce_start(stage, value):
        red_out[stage] = value
        at = sum(len(group) for group in stages[:stage])
        return [
            send(red_out.at[stage], red_in.at[at + i], other)
            for i, other in enumerate(stages[stage])
        ]

    def reduce_finish(stage, copies, value):
        for copy in copies:
            copy.wait()
        at = sum(len(group) for group in stages[:stage])
        for i in range(len(copies)):
            value = value + red_in[at + i]
        return value

    acc[...] = jnp.zeros_like(acc)
    going = reduce_start(0, tile)
    scatter(0, 6)
    tile = reduce_finish(0, going, tile)
    going = reduce_start(1, tile)
    scatter(6, 12)
    tile = reduce_finish(1, going, tile)
    going = reduce_start(2, tile)
    scatter(12, PAIRS)
    for k in range(ROWS):
        both = acc[16 * k : 16 * k + 8, :] + acc[16 * k + 8 : 16 * k + 16, :]
        if EDGE <= k < EDGE + OWN:
            extra = jnp.concatenate([diagonal(k - EDGE, t) for t in range(2)], axis=1)
            both = both + extra
        v_two[k] = both
    rims = [
        send(v_two.at[0:EDGE], rim_right.at[1, 0:EDGE], ring(-1)),
        send(v_two.at[ROWS - EDGE : ROWS], rim_left.at[1, 0:EDGE], ring(1)),
    ]
    tile = reduce_finish(2, going, tile)
    scalar = [
        jnp.sum(jnp.where(column == i, tile, 0.0), axis=1, keepdims=True) for i in range(4)
    ]
    gamma, a_sum, c_sum, d_sum = scalar
    step_one = gamma / a_sum
    fresh = gamma - 2.0 * step_one * a_sum + step_one * step_one * c_sum
    grow = 1.0 + fresh / gamma
    curve = grow * grow * a_sum - 2.0 * grow * step_one * c_sum + step_one * step_one * d_sum
    step_two = fresh / curve
    along = jnp.broadcast_to(step_one + step_two * grow, (VEC, 128))
    across = jnp.broadcast_to(step_one * step_two, (VEC, 128))
    for copy in rims:
        copy.wait()
    for k in range(EDGE):
        v_two[EDGE + k] = v_two[EDGE + k] + jnp.where(not_first, rim_left[1, k], 0.0)
        v_two[OWN + k] = v_two[OWN + k] + jnp.where(not_last, rim_right[1, k], 0.0)
    for k in range(OWN):
        for t in range(2):
            at = slice(128 * t, 128 * t + 128)
            col = slice(LANES * k + 128 * t, LANES * k + 128 * t + 128)
            r = rhs_ref[:, col]
            p = r * row(pre_ref, 2 * k + t)
            sol_ref[:, col] = along * p - across * win[EDGE + k, :, at]
            res_ref[:, col] = r - along * v_one[EDGE + k, :, at] + across * v_two[EDGE + k, :, at]


SENDS = 6 + 2 * 4 + 2 * 2 + 17


def on_device(
    rhs,
    potential,
    precond,
    shift,
    stiffness,
    cell_scale,
    conn,
    cell_count,
    projector,
    support_cell,
    support_atom,
    support_count,
    atom_matrix,
):
    vmem = pl.BlockSpec(memory_space=pltpu.VMEM)
    smem = pl.BlockSpec(memory_space=pltpu.SMEM)
    shape = jax.ShapeDtypeStruct((VEC, NODE_DEV), F32)
    return pl.pallas_call(
        kernel,
        name="pcg",
        out_shape=(shape, shape),
        in_specs=[smem] * 6 + [vmem] * 7,
        out_specs=(vmem, vmem),
        scratch_shapes=[
            pltpu.VMEM((ROWS, VEC, LANES), F32),
            pltpu.VMEM((ROWS * VEC, 2 * LANES), BF16),
            pltpu.VMEM((PAIRS, LANES, 2 * PAD), BF16),
            pltpu.VMEM((CELLS, 1, PAD), jnp.int32),
            pltpu.VMEM((CELLS, VEC, PAD), F32),
            pltpu.VMEM((PAIRS, 16, PAD), BF16),
            pltpu.VMEM((PAIRS, 16, PAD), BF16),
            pltpu.VMEM((PAD, PAD), BF16),
            pltpu.VMEM((PAD, PAD), BF16),
            pltpu.VMEM((ENTRIES * NPROJ, PAD), F32),
            pltpu.VMEM((CELLS, PAD), jnp.int32),
            pltpu.VMEM((CELLS, VEC, PAD), F32),
            pltpu.VMEM((CELLS, 16, PAD), BF16),
            pltpu.VMEM((ROWS * 16, LANES), F32),
            pltpu.VMEM((ROWS, VEC, LANES), F32),
            pltpu.VMEM((ROWS, VEC, LANES), F32),
            pltpu.VMEM((2, 2 * EDGE, VEC, LANES), F32),
            pltpu.VMEM((2, 2 * EDGE, VEC, LANES), F32),
            pltpu.VMEM((2, 8, 128), F32),
            pltpu.VMEM((2, 8, 128), F32),
            pltpu.VMEM((2, OWNED * NPROJ, NPROJ), F32),
            pltpu.VMEM((2, 3 * OWNED, VEC, 128), F32),
            pltpu.VMEM((2, 2, VEC, 128), F32),
            pltpu.VMEM((2, 4, VEC, 128), F32),
            pltpu.VMEM((2, 4, VEC, 128), F32),
            pltpu.VMEM((2, 2, VEC, 128), F32),
            pltpu.VMEM((3, VEC, 128), F32),
            pltpu.VMEM((17, VEC, 128), F32),
            pltpu.SemaphoreType.DMA((SENDS,)),
            pltpu.SemaphoreType.DMA((SENDS,)),
        ],
        compiler_params=pltpu.CompilerParams(
            collective_id=0, has_side_effects=True, vmem_limit_bytes=40 << 20
        ),
    )(
        cell_count,
        support_cell,
        support_atom,
        support_count,
        shift,
        cell_scale,
        rhs,
        potential.reshape(52, 128),
        precond.reshape(52, 128),
        stiffness,
        conn,
        projector.reshape(ENTRIES * NPROJ, ELEM),
        atom_matrix.reshape(OWNED * NPROJ, NPROJ),
    )


def solution(mesh):
    in_specs = (
        P(None, "dom"),
        P("dom"),
        P("dom"),
        P(),
        P(),
        P("dom"),
        P("dom", None),
        P(),
        P("dom", None, None),
        P("dom"),
        P("dom"),
        P(),
        P("dom", None, None),
    )
    out_specs = (P(None, "dom"), P(None, "dom"))
    return jax.shard_map(
        on_device, mesh=mesh, in_specs=in_specs, out_specs=out_specs, check_vma=False
    )
```

```python
import jax
import jax.numpy as jnp
from jax import lax
from jax.experimental import pallas as pl
from jax.experimental.pallas import tpu as pltpu
from jax.sharding import PartitionSpec as P

F32 = jnp.float32
BF16 = jnp.bfloat16
HIGH = lax.Precision.HIGHEST
MESH = pl.DeviceIdType.MESH

VEC = 8
NPROJ = 8
ELEM = 343
PAD = 384
CELLS = 32
PAIRS = CELLS // 2
ENTRIES = 8
SLOTS = CELLS + ENTRIES
SLOT_PAIRS = SLOTS // 2
OWNED = 2
NODE_DEV = 6656
GHOST = 416
LANES = 256
OWN = NODE_DEV // LANES
EDGE = 2
ROWS = OWN + 2 * EDGE
SHIFT = EDGE * LANES - GHOST
N_DOM = 256


def kernel(
    count_ref,
    support_cell_ref,
    support_atom_ref,
    support_count_ref,
    shift_ref,
    scale_ref,
    rhs_hbm,
    pot_hbm,
    pre_hbm,
    stiff_hbm,
    conn_hbm,
    proj_hbm,
    atom_hbm,
    sol_ref,
    res_ref,
    rhs_ref,
    pot_ref,
    pre_ref,
    stiff_ref,
    conn_ref,
    proj_ref,
    atom_ref,
    win,
    split_main,
    split_rim,
    onehot,
    pos_ref,
    hi_ref,
    hi_wide,
    values,
    lhs_hi,
    lhs_lo,
    stiff_hi,
    stiff_lo,
    proj_pad,
    spread_ref,
    packed,
    acc,
    v_one,
    v_two,
    rim_left,
    rim_right,
    pre_out,
    pre_in,
    atom_in,
    coef_out,
    coef_m2,
    coef_m1,
    coef_p1,
    coef_p2,
    red_out,
    red_in,
    load_sem,
    send_sem,
    recv_sem,
):
    me = lax.axis_index("dom")

    def ring(step):
        return lax.rem(me + (step + N_DOM), N_DOM)

    low16 = lax.rem(me, 16)
    high16 = lax.div(me, 16)
    stages = (
        [me - low16 + lax.rem(low16 + d, 16) for d in range(1, 16)],
        [low16 + 16 * lax.rem(high16 + d, 16) for d in range(1, 16)],
    )
    greeted = [ring(-2), ring(-1), ring(1), ring(2)]
    for group in stages:
        greeted = greeted + group
    barrier = pltpu.get_barrier_semaphore()
    for other in greeted:
        pl.semaphore_signal(barrier, inc=1, device_id=(other,), device_id_type=MESH)

    loads = []
    for i, (src, dst) in enumerate(
        (
            (conn_hbm, conn_ref),
            (rhs_hbm, rhs_ref),
            (pre_hbm, pre_ref),
            (atom_hbm, atom_ref),
            (proj_hbm, proj_ref),
            (stiff_hbm, stiff_ref),
            (pot_hbm, pot_ref),
        )
    ):
        load = pltpu.make_async_copy(src, dst, load_sem.at[i])
        load.start()
        loads.append(load)

    used = [0]

    def send(src, dst, target):
        slot = used[0]
        used[0] = slot + 1
        copy = pltpu.make_async_remote_copy(
            src_ref=src,
            dst_ref=dst,
            send_sem=send_sem.at[slot],
            recv_sem=recv_sem.at[slot],
            device_id=(target,),
            device_id_type=MESH,
        )
        copy.start()
        return copy

    def row(ref, index):
        return jnp.broadcast_to(ref[index : index + 1, :], (VEC, 128))

    for load in loads[1:4]:
        load.wait()
    dot_acc = jnp.zeros((VEC, 128), F32)
    for k in range(OWN):
        for t in range(2):
            column = LANES * k + 128 * t
            r = rhs_ref[:, column : column + 128]
            p = r * row(pre_ref, 2 * k + t)
            win[EDGE + k, :, 128 * t : 128 * t + 128] = p
            dot_acc = dot_acc + r * p
    gamma = jnp.sum(dot_acc, axis=1, keepdims=True)
    pre_out[...] = jnp.zeros_like(pre_out)
    pre_out[0, 0:4, :] = pre_ref[0:4, :]
    pre_out[1, 0:4, :] = pre_ref[48:52, :]
    pl.semaphore_wait(barrier, len(greeted))
    first = [
        send(win.at[EDGE : 2 * EDGE], win.at[ROWS - EDGE : ROWS], ring(-1)),
        send(win.at[OWN : OWN + EDGE], win.at[0:EDGE], ring(1)),
        send(pre_out.at[0], pre_in.at[1], ring(-1)),
        send(pre_out.at[1], pre_in.at[0], ring(1)),
        send(atom_ref, atom_in.at[1], ring(-1)),
        send(atom_ref, atom_in.at[0], ring(1)),
    ]

    loads[0].wait()
    spread_ref[...] = jnp.full((CELLS, PAD), -1, jnp.int32)
    spread_ref[:, 0:ELEM] = conn_ref[...] + SHIFT
    for c in range(CELLS):
        pos_ref[c] = spread_ref[c : c + 1, :]
    for s in range(ENTRIES):
        pos_ref[CELLS + s] = pos_ref[support_cell_ref[s]]
    number = lax.broadcasted_iota(jnp.int32, (LANES, PAD), 0).astype(jnp.int16)

    def build(c, carry):
        for q in range(2):
            slot = 2 * c + q
            place = pos_ref[slot]
            high = jnp.right_shift(place, 8)
            hi_ref[slot] = high
            hi_wide[slot] = jnp.broadcast_to(high, (16, PAD)).astype(jnp.int16)
            low = jnp.bitwise_and(place, LANES - 1)
            low = jnp.broadcast_to(low, (16, PAD)).astype(jnp.int16)
            one = jnp.ones((16, PAD), BF16)
            zero = jnp.zeros((16, PAD), BF16)
            for r in range(LANES // 16):
                hit = jnp.where(number[16 * r : 16 * r + 16, :] == low, one, zero)
                onehot[c, 16 * r : 16 * r + 16, PAD * q : PAD * q + PAD] = hit
        return carry

    lax.fori_loop(0, SLOT_PAIRS, build, 0)

    live_cells = count_ref[me]

    def split(block):
        up = block.astype(BF16)
        return up, (block - up.astype(F32)).astype(BF16)

    def gather_main(blocks):
        count = len(blocks) * VEC
        for i, k in enumerate(blocks):
            up, down = split(win[k])
            split_main[0, VEC * i : VEC * i + VEC, :] = up
            split_main[1, VEC * i : VEC * i + VEC, :] = down

        def body(c, carry):
            oh = onehot[c]
            g = jnp.dot(split_main[0, 0:count, :], oh, preferred_element_type=F32) + jnp.dot(
                split_main[1, 0:count, :], oh, preferred_element_type=F32
            )
            for q in range(2):
                for t in range(3):
                    h = jnp.broadcast_to(
                        hi_ref[2 * c + q, :, 128 * t : 128 * t + 128], (VEC, 128)
                    )
                    got = jnp.zeros((VEC, 128), F32)
                    at = PAD * q + 128 * t
                    for i, k in enumerate(blocks):
                        got = jnp.where(h == k, g[VEC * i : VEC * i + VEC, at : at + 128], got)
                    values[2 * c + q, :, 128 * t : 128 * t + 128] = got
            return carry

        lax.fori_loop(0, SLOT_PAIRS, body, 0, unroll=4)

    def prepare_rim(blocks):
        count = len(blocks) * VEC
        for i, k in enumerate(blocks):
            up, down = split(win[k])
            split_rim[VEC * i : VEC * i + VEC, :] = up
            split_rim[count + VEC * i : count + VEC * i + VEC, :] = down

    def gather_rim(blocks, first_pair, last_pair, cells):
        count = len(blocks) * VEC

        def body(c, carry):
            g = jnp.dot(split_rim[0 : 2 * count, :], onehot[c], preferred_element_type=F32)
            g = g[0:count] + g[count : 2 * count]
            ups, downs = [], []
            for q in range(2):
                slot = 2 * c + q
                parts = []
                for t in range(3):
                    h = jnp.broadcast_to(hi_ref[slot, :, 128 * t : 128 * t + 128], (VEC, 128))
                    got = values[slot, :, 128 * t : 128 * t + 128]
                    at = PAD * q + 128 * t
                    for i, k in enumerate(blocks):
                        got = jnp.where(h == k, g[VEC * i : VEC * i + VEC, at : at + 128], got)
                    parts.append(got)
                full = jnp.concatenate(parts, axis=1)
                values[slot] = full
                if cells:
                    weight = jnp.where(slot < live_cells, scale_ref[slot], 0.0)
                    up, down = split(full * weight)
                    ups.append(up)
                    downs.append(down)
            if cells:
                lhs_hi[c] = jnp.concatenate(ups, axis=0)
                lhs_lo[c] = jnp.concatenate(downs, axis=0)
            return carry

        lax.fori_loop(first_pair, last_pair, body, 0, unroll=4)

    def scatter(first_pair, last_pair):
        def body(c, carry):
            v = jnp.concatenate([packed[2 * c], packed[2 * c + 1]], axis=1)
            h = jnp.concatenate([hi_wide[2 * c], hi_wide[2 * c + 1]], axis=1)
            zero = jnp.zeros_like(v)
            a = jnp.concatenate([jnp.where(h == k, v, zero) for k in range(ROWS)], axis=0)
            acc[...] += lax.dot_general(
                a, onehot[c], (((1,), (1,)), ((), ())), preferred_element_type=F32
            )
            return carry

        lax.fori_loop(first_pair, last_pair, body, 0, unroll=4)

    own_blocks = list(range(EDGE, EDGE + OWN))
    ghost_blocks = list(range(EDGE)) + list(range(EDGE + OWN, ROWS))
    inner_blocks = list(range(2 * EDGE, OWN))
    rim_blocks = list(range(2 * EDGE)) + list(range(OWN, ROWS))

    gather_main(own_blocks)

    for load in loads[4:]:
        load.wait()
    stiff_hi[...] = jnp.zeros_like(stiff_hi)
    stiff_lo[...] = jnp.zeros_like(stiff_lo)
    up, down = split(stiff_ref[...])
    stiff_hi[0:ELEM, 0:ELEM] = up
    stiff_lo[0:ELEM, 0:ELEM] = down
    proj_pad[...] = jnp.zeros_like(proj_pad)
    proj_pad[:, 0:ELEM] = proj_ref[...]

    lane64 = lax.broadcasted_iota(jnp.int32, (1, 64), 1)
    entry_of = jnp.right_shift(lane64, 3)
    live_entries = support_count_ref[me]
    atom_row = jnp.full((1, 64), -1, jnp.int32)
    relative = []
    for s in range(ENTRIES):
        own_atom = jnp.where(s < live_entries, support_atom_ref[s] - (me - 1) * OWNED, -1)
        relative.append(own_atom)
        atom_row = jnp.where(entry_of == s, own_atom, atom_row)
    sublane = lax.broadcasted_iota(jnp.int32, (VEC, 128), 0)
    shift_col = jnp.zeros((VEC, 128), F32)
    for v in range(VEC):
        shift_col = jnp.where(sublane == v, shift_ref[v], shift_col)
    r64 = lax.broadcasted_iota(jnp.int32, (64, 48), 0)
    c48 = lax.broadcasted_iota(jnp.int32, (64, 48), 1)
    fold = jnp.where(jnp.bitwise_and(r64, 7) == jnp.bitwise_and(c48, 7), 1.0, 0.0).astype(F32)
    r48 = lax.broadcasted_iota(jnp.int32, (48, 48), 0)
    d48 = lax.broadcasted_iota(jnp.int32, (48, 48), 1)
    same_atom = jnp.right_shift(r48, 3) == jnp.right_shift(d48, 3)
    r8 = lax.broadcasted_iota(jnp.int32, (8, 64), 0)
    c64 = lax.broadcasted_iota(jnp.int32, (8, 64), 1)
    tile8 = jnp.where(r8 == jnp.bitwise_and(c64, 7), 1.0, 0.0).astype(F32)
    for copy in first:
        copy.wait()
    not_first = me > 0
    not_last = me < N_DOM - 1
    for k in range(EDGE):
        win[k] = jnp.where(not_first, win[k], 0.0)
        win[ROWS - EDGE + k] = jnp.where(not_last, win[ROWS - EDGE + k], 0.0)
    atoms = jnp.concatenate([atom_in[0], atom_ref[...], atom_in[1]], axis=0)
    atom_tiled = jnp.dot(atoms, tile8, precision=HIGH, preferred_element_type=F32)

    def coef_start(step):
        picked = values[CELLS:SLOTS].reshape(ENTRIES * VEC, PAD)
        cross = lax.dot_general(
            picked,
            proj_pad[...],
            (((1,), (1,)), ((), ())),
            precision=HIGH,
            preferred_element_type=F32,
        )
        own = [jnp.zeros((VEC, 64), F32) for _ in range(3 * OWNED)]
        for s in range(ENTRIES):
            mine = jnp.where(entry_of == s, cross[VEC * s : VEC * s + VEC, :], 0.0)
            for a in range(3 * OWNED):
                own[a] = own[a] + jnp.where(relative[s] == a, mine, 0.0)
        for a in range(3 * OWNED):
            coef_out[step, a, :, 0:64] = own[a]
        copies = [
            send(coef_out.at[step, 0:4], coef_p1.at[step], ring(-1)),
            send(coef_out.at[step, 2:6], coef_m1.at[step], ring(1)),
            send(coef_out.at[step, 0:2], coef_p2.at[step], ring(-2)),
            send(coef_out.at[step, 4:6], coef_m2.at[step], ring(2)),
        ]
        return copies

    def coef_finish(step, copies):
        for copy in copies:
            copy.wait()
        own = coef_out[step, :, :, 0:64]
        left2, left1 = coef_m2[step, :, :, 0:64], coef_m1[step, :, :, 0:64]
        right1, right2 = coef_p1[step, :, :, 0:64], coef_p2[step, :, :, 0:64]
        total = [
            own[0] + left1[0] + left2[0],
            own[1] + left1[1] + left2[1],
            own[2] + left1[2] + right1[0],
            own[3] + left1[3] + right1[1],
            own[4] + right1[2] + right2[0],
            own[5] + right1[3] + right2[1],
        ]
        stacked = jnp.concatenate(total, axis=0)
        coef = jnp.dot(stacked, fold, precision=HIGH, preferred_element_type=F32)
        coef = jnp.where(same_atom, coef, 0.0)
        term = jnp.dot(coef, atom_tiled, precision=HIGH, preferred_element_type=F32)
        both = coef[2 * VEC : 4 * VEC, :] * term[2 * VEC : 4 * VEC, 0:48]
        energy = jnp.sum(both[0:VEC] + both[VEC : 2 * VEC], axis=1, keepdims=True)
        return term, energy

    def support_products(term):
        chosen = jnp.zeros((VEC, 64), F32)
        for a in range(3 * OWNED):
            chosen = chosen + jnp.where(atom_row == a, term[VEC * a : VEC * a + VEC, :], 0.0)
        back = jnp.concatenate(
            [jnp.where(entry_of == s, chosen, 0.0) for s in range(ENTRIES)], axis=0
        )
        out = jnp.dot(back, proj_pad[...], precision=HIGH, preferred_element_type=F32)
        for s in range(ENTRIES):
            up, down = split(out[VEC * s : VEC * s + VEC, :])
            packed[CELLS + s] = jnp.concatenate([up, down], axis=0)

    def cell_products():
        uh = lhs_hi[...].reshape(CELLS * VEC, PAD)
        ul = lhs_lo[...].reshape(CELLS * VEC, PAD)
        out = jnp.dot(uh, stiff_hi[...], preferred_element_type=F32)
        out = out + jnp.dot(uh, stiff_lo[...], preferred_element_type=F32)
        out = out + jnp.dot(ul, stiff_hi[...], preferred_element_type=F32)
        energy = jnp.zeros((VEC, PAD), F32)
        for c in range(CELLS):
            full = out[VEC * c : VEC * c + VEC, :]
            up, down = split(full)
            packed[c] = jnp.concatenate([up, down], axis=0)
            energy = energy + full * values[c]
        return energy

    def assembled(k):
        both = acc[16 * k : 16 * k + 8, :] + acc[16 * k + 8 : 16 * k + 16, :]
        if EDGE <= k < EDGE + OWN:
            extra = []
            for t in range(2):
                diagonal = row(pot_ref, 2 * (k - EDGE) + t) + shift_col
                extra.append(diagonal * win[k, :, 128 * t : 128 * t + 128])
            both = both + jnp.concatenate(extra, axis=1)
        return both

    prepare_rim(ghost_blocks)
    gather_rim(ghost_blocks, PAIRS, SLOT_PAIRS, False)
    coefs = coef_start(0)
    gather_rim(ghost_blocks, 0, PAIRS, True)
    cell_products()
    acc[...] = jnp.zeros_like(acc)
    scatter(0, PAIRS)
    term, _ = coef_finish(0, coefs)
    support_products(term)
    scatter(PAIRS, SLOT_PAIRS)
    for k in rim_blocks:
        v_one[k] = assembled(k)
    rims = [
        send(v_one.at[0 : 2 * EDGE], rim_right.at[0], ring(-1)),
        send(v_one.at[OWN:ROWS], rim_left.at[0], ring(1)),
    ]
    for k in inner_blocks:
        v_one[k] = assembled(k)

    sums = [jnp.zeros((VEC, 128), F32) for _ in range(3)]

    def advance(k, sums):
        a_acc, c_acc, d_acc = sums
        for t in range(2):
            at = slice(128 * t, 128 * t + 128)
            index = 2 * (k - EDGE) + t
            image = v_one[k, :, at]
            a_acc = a_acc + image * win[k, :, at]
            w = image * row(pre_ref, index)
            win[k, :, at] = w
            c_acc = c_acc + image * w
            d_acc = d_acc + (row(pot_ref, index) + shift_col) * w * w
        return [a_acc, c_acc, d_acc]

    for k in inner_blocks:
        sums = advance(k, sums)
    gather_main(inner_blocks)
    for copy in rims:
        copy.wait()
    for k in range(2 * EDGE):
        v_one[k] = v_one[k] + jnp.where(not_first, rim_left[0, k], 0.0)
        v_one[OWN + k] = v_one[OWN + k] + jnp.where(not_last, rim_right[0, k], 0.0)
    for k in rim_blocks:
        if EDGE <= k < EDGE + OWN:
            sums = advance(k, sums)
    for k in range(EDGE):
        for t in range(2):
            at = slice(128 * t, 128 * t + 128)
            left = row(pre_in.at[0], 2 * k + t) * v_one[k, :, at]
            win[k, :, at] = jnp.where(not_first, left, 0.0)
            right = row(pre_in.at[1], 2 * k + t) * v_one[OWN + EDGE + k, :, at]
            win[OWN + EDGE + k, :, at] = jnp.where(not_last, right, 0.0)

    prepare_rim(rim_blocks)
    gather_rim(rim_blocks, PAIRS, SLOT_PAIRS, False)
    coefs = coef_start(1)
    gather_rim(rim_blocks, 0, PAIRS, True)
    energy = cell_products()
    acc[...] = jnp.zeros_like(acc)
    scatter(0, 12)
    term, support_energy = coef_finish(1, coefs)

    a_acc, c_acc, d_acc = sums
    for t in range(3):
        d_acc = d_acc + energy[:, 128 * t : 128 * t + 128]
    column = lax.broadcasted_iota(jnp.int32, (VEC, 128), 1)
    tile = jnp.zeros((VEC, 128), F32)
    locals_ = (
        gamma,
        jnp.sum(a_acc, axis=1, keepdims=True),
        jnp.sum(c_acc, axis=1, keepdims=True),
        jnp.sum(d_acc, axis=1, keepdims=True) + support_energy,
    )
    for i, value in enumerate(locals_):
        tile = jnp.where(column == i, value, tile)

    def reduce_start(stage, value):
        red_out[stage] = value
        return [
            send(red_out.at[stage], red_in.at[15 * stage + i], other)
            for i, other in enumerate(stages[stage])
        ]

    def reduce_finish(stage, copies, value):
        for copy in copies:
            copy.wait()
        for i in range(len(copies)):
            value = value + red_in[15 * stage + i]
        return value

    going = reduce_start(0, tile)
    support_products(term)
    scatter(12, SLOT_PAIRS)
    for k in rim_blocks:
        v_two[k] = assembled(k)
    rims = [
        send(v_two.at[0:EDGE], rim_right.at[1, 0:EDGE], ring(-1)),
        send(v_two.at[ROWS - EDGE : ROWS], rim_left.at[1, 0:EDGE], ring(1)),
    ]
    tile = reduce_finish(0, going, tile)
    going = reduce_start(1, tile)
    for k in inner_blocks:
        v_two[k] = assembled(k)
    for copy in rims:
        copy.wait()
    for k in range(EDGE):
        v_two[EDGE + k] = v_two[EDGE + k] + jnp.where(not_first, rim_left[1, k], 0.0)
        v_two[OWN + k] = v_two[OWN + k] + jnp.where(not_last, rim_right[1, k], 0.0)
    tile = reduce_finish(1, going, tile)
    gamma, a_sum, c_sum, d_sum = [
        jnp.sum(jnp.where(column == i, tile, 0.0), axis=1, keepdims=True) for i in range(4)
    ]
    step_one = gamma / a_sum
    fresh = gamma - 2.0 * step_one * a_sum + step_one * step_one * c_sum
    grow = 1.0 + fresh / gamma
    curve = grow * grow * a_sum - 2.0 * grow * step_one * c_sum + step_one * step_one * d_sum
    step_two = fresh / curve
    along = jnp.broadcast_to(step_one + step_two * grow, (VEC, 128))
    across = jnp.broadcast_to(step_one * step_two, (VEC, 128))
    for k in range(OWN):
        for t in range(2):
            at = slice(128 * t, 128 * t + 128)
            col = slice(LANES * k + 128 * t, LANES * k + 128 * t + 128)
            r = rhs_ref[:, col]
            p = r * row(pre_ref, 2 * k + t)
            sol_ref[:, col] = along * p - across * win[EDGE + k, :, at]
            res_ref[:, col] = r - along * v_one[EDGE + k, :, at] + across * v_two[EDGE + k, :, at]


SENDS = 6 + 2 * 4 + 2 * 2 + 30


def on_device(
    rhs,
    potential,
    precond,
    shift,
    stiffness,
    cell_scale,
    conn,
    cell_count,
    projector,
    support_cell,
    support_atom,
    support_count,
    atom_matrix,
):
    vmem = pl.BlockSpec(memory_space=pltpu.VMEM)
    smem = pl.BlockSpec(memory_space=pltpu.SMEM)
    shape = jax.ShapeDtypeStruct((VEC, NODE_DEV), F32)
    return pl.pallas_call(
        kernel,
        name="pcg",
        out_shape=(shape, shape),
        in_specs=[smem] * 6 + [pl.BlockSpec(memory_space=pltpu.HBM)] * 7,
        out_specs=(vmem, vmem),
        scratch_shapes=[
            pltpu.VMEM((VEC, NODE_DEV), F32),
            pltpu.VMEM((52, 128), F32),
            pltpu.VMEM((52, 128), F32),
            pltpu.VMEM((ELEM, ELEM), F32),
            pltpu.VMEM((CELLS, ELEM), jnp.int32),
            pltpu.VMEM((ENTRIES * NPROJ, ELEM), F32),
            pltpu.VMEM((OWNED * NPROJ, NPROJ), F32),
            pltpu.VMEM((ROWS, VEC, LANES), F32),
            pltpu.VMEM((2, ROWS * VEC, LANES), BF16),
            pltpu.VMEM((4 * EDGE * VEC * 2, LANES), BF16),
            pltpu.VMEM((SLOT_PAIRS, LANES, 2 * PAD), BF16),
            pltpu.VMEM((SLOTS, 1, PAD), jnp.int32),
            pltpu.VMEM((SLOTS, 1, PAD), jnp.int32),
            pltpu.VMEM((SLOTS, 16, PAD), jnp.int16),
            pltpu.VMEM((SLOTS, VEC, PAD), F32),
            pltpu.VMEM((PAIRS, 16, PAD), BF16),
            pltpu.VMEM((PAIRS, 16, PAD), BF16),
            pltpu.VMEM((PAD, PAD), BF16),
            pltpu.VMEM((PAD, PAD), BF16),
            pltpu.VMEM((ENTRIES * NPROJ, PAD), F32),
            pltpu.VMEM((CELLS, PAD), jnp.int32),
            pltpu.VMEM((SLOTS, 16, PAD), BF16),
            pltpu.VMEM((ROWS * 16, LANES), F32),
            pltpu.VMEM((ROWS, VEC, LANES), F32),
            pltpu.VMEM((ROWS, VEC, LANES), F32),
            pltpu.VMEM((2, 2 * EDGE, VEC, LANES), F32),
            pltpu.VMEM((2, 2 * EDGE, VEC, LANES), F32),
            pltpu.VMEM((2, 8, 128), F32),
            pltpu.VMEM((2, 8, 128), F32),
            pltpu.VMEM((2, OWNED * NPROJ, NPROJ), F32),
            pltpu.VMEM((2, 3 * OWNED, VEC, 128), F32),
            pltpu.VMEM((2, 2, VEC, 128), F32),
            pltpu.VMEM((2, 4, VEC, 128), F32),
            pltpu.VMEM((2, 4, VEC, 128), F32),
            pltpu.VMEM((2, 2, VEC, 128), F32),
            pltpu.VMEM((2, VEC, 128), F32),
            pltpu.VMEM((30, VEC, 128), F32),
            pltpu.SemaphoreType.DMA((7,)),
            pltpu.SemaphoreType.DMA((SENDS,)),
            pltpu.SemaphoreType.DMA((SENDS,)),
        ],
        compiler_params=pltpu.CompilerParams(
            collective_id=0, has_side_effects=True, vmem_limit_bytes=32 << 20
        ),
    )(
        cell_count,
        support_cell,
        support_atom,
        support_count,
        shift,
        cell_scale,
        rhs,
        potential.reshape(52, 128),
        precond.reshape(52, 128),
        stiffness,
        conn,
        projector.reshape(ENTRIES * NPROJ, ELEM),
        atom_matrix.reshape(OWNED * NPROJ, NPROJ),
    )


def solution(mesh):
    in_specs = (
        P(None, "dom"),
        P("dom"),
        P("dom"),
        P(),
        P(),
        P("dom"),
        P("dom", None),
        P(),
        P("dom", None, None),
        P("dom"),
        P("dom"),
        P(),
        P("dom", None, None),
    )
    out_specs = (P(None, "dom"), P(None, "dom"))
    return jax.shard_map(
        on_device, mesh=mesh, in_specs=in_specs, out_specs=out_specs, check_vma=False
    )
```

```python
import jax
import jax.numpy as jnp
from jax import lax
from jax.experimental import pallas as pl
from jax.experimental.pallas import tpu as pltpu
from jax.sharding import PartitionSpec as P

F32 = jnp.float32
BF16 = jnp.bfloat16
HIGH = lax.Precision.HIGHEST
MESH = pl.DeviceIdType.MESH

VEC = 8
NPROJ = 8
ELEM = 343
PAD = 384
CELLS = 32
PAIRS = CELLS // 2
ENTRIES = 8
SLOTS = CELLS + ENTRIES
SLOT_PAIRS = SLOTS // 2
OWNED = 2
NODE_DEV = 6656
GHOST = 416
LANES = 256
OWN = NODE_DEV // LANES
EDGE = 2
ROWS = OWN + 2 * EDGE
SHIFT = EDGE * LANES - GHOST
N_DOM = 256


def kernel(
    count_ref,
    support_cell_ref,
    support_atom_ref,
    support_count_ref,
    shift_ref,
    scale_ref,
    rhs_hbm,
    pot_hbm,
    pre_hbm,
    stiff_hbm,
    conn_hbm,
    proj_hbm,
    atom_hbm,
    sol_ref,
    res_ref,
    rhs_ref,
    pot_ref,
    pre_ref,
    stiff_ref,
    conn_ref,
    proj_ref,
    atom_ref,
    win,
    split_main,
    split_rim,
    onehot,
    pos_ref,
    hi_ref,
    hi_wide,
    values,
    lhs_hi,
    lhs_lo,
    stiff_hi,
    stiff_lo,
    proj_pad,
    spread_ref,
    packed,
    acc,
    v_one,
    v_two,
    rim_left,
    rim_right,
    pre_out,
    pre_in,
    atom_in,
    coef_out,
    coef_m2,
    coef_m1,
    coef_p1,
    coef_p2,
    red_out,
    red_in,
    load_sem,
    send_sem,
    recv_sem,
):
    me = lax.axis_index("dom")

    def ring(step):
        return lax.rem(me + (step + N_DOM), N_DOM)

    low16 = lax.rem(me, 16)
    high16 = lax.div(me, 16)
    stages = (
        [me - low16 + lax.rem(low16 + d, 16) for d in range(1, 16)],
        [low16 + 16 * lax.rem(high16 + d, 16) for d in range(1, 16)],
    )
    greeted = [ring(-2), ring(-1), ring(1), ring(2)]
    for group in stages:
        greeted = greeted + group
    barrier = pltpu.get_barrier_semaphore()
    for other in greeted:
        pl.semaphore_signal(barrier, inc=1, device_id=(other,), device_id_type=MESH)

    loads = []
    for i, (src, dst) in enumerate(
        (
            (conn_hbm, conn_ref),
            (rhs_hbm, rhs_ref),
            (pre_hbm, pre_ref),
            (atom_hbm, atom_ref),
            (proj_hbm, proj_ref),
            (stiff_hbm, stiff_ref),
            (pot_hbm, pot_ref),
        )
    ):
        load = pltpu.make_async_copy(src, dst, load_sem.at[i])
        load.start()
        loads.append(load)

    used = [0]

    def send(src, dst, target):
        slot = used[0]
        used[0] = slot + 1
        copy = pltpu.make_async_remote_copy(
            src_ref=src,
            dst_ref=dst,
            send_sem=send_sem.at[slot],
            recv_sem=recv_sem.at[slot],
            device_id=(target,),
            device_id_type=MESH,
        )
        copy.start()
        return copy

    def row(ref, index):
        return jnp.broadcast_to(ref[index : index + 1, :], (VEC, 128))

    def wide_row(ref, k):
        return jnp.concatenate([row(ref, 2 * k), row(ref, 2 * k + 1)], axis=1)

    for load in loads[1:4]:
        load.wait()
    dot_acc = jnp.zeros((VEC, 128), F32)
    for k in range(OWN):
        for t in range(2):
            column = LANES * k + 128 * t
            r = rhs_ref[:, column : column + 128]
            p = r * row(pre_ref, 2 * k + t)
            win[EDGE + k, :, 128 * t : 128 * t + 128] = p
            dot_acc = dot_acc + r * p
    gamma = jnp.sum(dot_acc, axis=1, keepdims=True)
    pre_out[...] = jnp.zeros_like(pre_out)
    pre_out[0, 0:4, :] = pre_ref[0:4, :]
    pre_out[1, 0:4, :] = pre_ref[48:52, :]
    pl.semaphore_wait(barrier, len(greeted))
    first = [
        send(win.at[EDGE : 2 * EDGE], win.at[ROWS - EDGE : ROWS], ring(-1)),
        send(win.at[OWN : OWN + EDGE], win.at[0:EDGE], ring(1)),
        send(pre_out.at[0], pre_in.at[1], ring(-1)),
        send(pre_out.at[1], pre_in.at[0], ring(1)),
        send(atom_ref, atom_in.at[1], ring(-1)),
        send(atom_ref, atom_in.at[0], ring(1)),
    ]

    loads[0].wait()
    spread_ref[...] = jnp.full((CELLS, PAD), -1, jnp.int32)
    spread_ref[:, 0:ELEM] = conn_ref[...] + SHIFT
    for c in range(CELLS):
        pos_ref[c] = spread_ref[c : c + 1, :]
    for s in range(ENTRIES):
        pos_ref[CELLS + s] = pos_ref[support_cell_ref[s]]
    number = lax.broadcasted_iota(jnp.int32, (LANES, PAD), 0).astype(jnp.int16)

    def build(c, carry):
        for q in range(2):
            slot = 2 * c + q
            place = pos_ref[slot]
            high = jnp.right_shift(place, 8)
            hi_ref[slot] = high
            hi_wide[slot] = jnp.broadcast_to(high, (16, PAD)).astype(jnp.int16)
            low = jnp.bitwise_and(place, LANES - 1)
            low = jnp.broadcast_to(low, (16, PAD)).astype(jnp.int16)
            one = jnp.ones((16, PAD), BF16)
            zero = jnp.zeros((16, PAD), BF16)
            for r in range(LANES // 16):
                hit = jnp.where(number[16 * r : 16 * r + 16, :] == low, one, zero)
                onehot[c, 16 * r : 16 * r + 16, PAD * q : PAD * q + PAD] = hit
        return carry

    lax.fori_loop(0, SLOT_PAIRS, build, 0)

    live_cells = count_ref[me]

    def split(block):
        up = block.astype(BF16)
        return up, (block - up.astype(F32)).astype(BF16)

    def gather_main(blocks):
        count = len(blocks) * VEC
        for i, k in enumerate(blocks):
            up, down = split(win[k])
            split_main[0, VEC * i : VEC * i + VEC, :] = up
            split_main[1, VEC * i : VEC * i + VEC, :] = down

        def body(c, carry):
            oh = onehot[c]
            g = jnp.dot(split_main[0, 0:count, :], oh, preferred_element_type=F32) + jnp.dot(
                split_main[1, 0:count, :], oh, preferred_element_type=F32
            )
            for q in range(2):
                for t in range(3):
                    h = jnp.broadcast_to(
                        hi_ref[2 * c + q, :, 128 * t : 128 * t + 128], (VEC, 128)
                    )
                    got = jnp.zeros((VEC, 128), F32)
                    at = PAD * q + 128 * t
                    for i, k in enumerate(blocks):
                        got = jnp.where(h == k, g[VEC * i : VEC * i + VEC, at : at + 128], got)
                    values[2 * c + q, :, 128 * t : 128 * t + 128] = got
            return carry

        lax.fori_loop(0, SLOT_PAIRS, body, 0, unroll=4)

    def prepare_rim(blocks):
        count = len(blocks) * VEC
        for i, k in enumerate(blocks):
            up, down = split(win[k])
            split_rim[VEC * i : VEC * i + VEC, :] = up
            split_rim[count + VEC * i : count + VEC * i + VEC, :] = down

    def gather_rim(blocks, first_pair, last_pair, cells):
        count = len(blocks) * VEC

        def body(c, carry):
            g = jnp.dot(split_rim[0 : 2 * count, :], onehot[c], preferred_element_type=F32)
            g = g[0:count] + g[count : 2 * count]
            ups, downs = [], []
            for q in range(2):
                slot = 2 * c + q
                parts = []
                for t in range(3):
                    h = jnp.broadcast_to(hi_ref[slot, :, 128 * t : 128 * t + 128], (VEC, 128))
                    got = values[slot, :, 128 * t : 128 * t + 128]
                    at = PAD * q + 128 * t
                    for i, k in enumerate(blocks):
                        got = jnp.where(h == k, g[VEC * i : VEC * i + VEC, at : at + 128], got)
                    parts.append(got)
                full = jnp.concatenate(parts, axis=1)
                values[slot] = full
                if cells:
                    weight = jnp.where(slot < live_cells, scale_ref[slot], 0.0)
                    up, down = split(full * weight)
                    ups.append(up)
                    downs.append(down)
            if cells:
                lhs_hi[c] = jnp.concatenate(ups, axis=0)
                lhs_lo[c] = jnp.concatenate(downs, axis=0)
            return carry

        lax.fori_loop(first_pair, last_pair, body, 0, unroll=4)

    def scatter(first_pair, last_pair):
        def body(c, carry):
            v = jnp.concatenate([packed[2 * c], packed[2 * c + 1]], axis=1)
            h = jnp.concatenate([hi_wide[2 * c], hi_wide[2 * c + 1]], axis=1)
            zero = jnp.zeros_like(v)
            a = jnp.concatenate([jnp.where(h == k, v, zero) for k in range(ROWS)], axis=0)
            acc[...] += lax.dot_general(
                a, onehot[c], (((1,), (1,)), ((), ())), preferred_element_type=F32
            )
            return carry

        lax.fori_loop(first_pair, last_pair, body, 0, unroll=4)

    own_blocks = list(range(EDGE, EDGE + OWN))
    ghost_blocks = list(range(EDGE)) + list(range(EDGE + OWN, ROWS))
    inner_blocks = list(range(2 * EDGE, OWN))
    rim_blocks = list(range(2 * EDGE)) + list(range(OWN, ROWS))

    gather_main(own_blocks)

    for load in loads[4:]:
        load.wait()
    stiff_hi[...] = jnp.zeros_like(stiff_hi)
    stiff_lo[...] = jnp.zeros_like(stiff_lo)
    up, down = split(stiff_ref[...])
    stiff_hi[0:ELEM, 0:ELEM] = up
    stiff_lo[0:ELEM, 0:ELEM] = down
    proj_pad[...] = jnp.zeros_like(proj_pad)
    proj_pad[:, 0:ELEM] = proj_ref[...]

    lane64 = lax.broadcasted_iota(jnp.int32, (1, 64), 1)
    entry_of = jnp.right_shift(lane64, 3)
    live_entries = support_count_ref[me]
    atom_row = jnp.full((1, 64), -1, jnp.int32)
    relative = []
    for s in range(ENTRIES):
        own_atom = jnp.where(s < live_entries, support_atom_ref[s] - (me - 1) * OWNED, -1)
        relative.append(own_atom)
        atom_row = jnp.where(entry_of == s, own_atom, atom_row)
    sublane = lax.broadcasted_iota(jnp.int32, (VEC, 128), 0)
    shift_col = jnp.zeros((VEC, 128), F32)
    for v in range(VEC):
        shift_col = jnp.where(sublane == v, shift_ref[v], shift_col)
    r64 = lax.broadcasted_iota(jnp.int32, (64, 48), 0)
    c48 = lax.broadcasted_iota(jnp.int32, (64, 48), 1)
    fold = jnp.where(jnp.bitwise_and(r64, 7) == jnp.bitwise_and(c48, 7), 1.0, 0.0).astype(F32)
    r48 = lax.broadcasted_iota(jnp.int32, (48, 48), 0)
    d48 = lax.broadcasted_iota(jnp.int32, (48, 48), 1)
    same_atom = jnp.right_shift(r48, 3) == jnp.right_shift(d48, 3)
    r8 = lax.broadcasted_iota(jnp.int32, (8, 64), 0)
    c64 = lax.broadcasted_iota(jnp.int32, (8, 64), 1)
    tile8 = jnp.where(r8 == jnp.bitwise_and(c64, 7), 1.0, 0.0).astype(F32)
    for copy in first:
        copy.wait()
    not_first = me > 0
    not_last = me < N_DOM - 1
    for k in range(EDGE):
        win[k] = jnp.where(not_first, win[k], 0.0)
        win[ROWS - EDGE + k] = jnp.where(not_last, win[ROWS - EDGE + k], 0.0)
    atoms = jnp.concatenate([atom_in[0], atom_ref[...], atom_in[1]], axis=0)
    atom_tiled = jnp.dot(atoms, tile8, precision=HIGH, preferred_element_type=F32)

    def coef_start(step):
        picked = values[CELLS:SLOTS].reshape(ENTRIES * VEC, PAD)
        cross = lax.dot_general(
            picked,
            proj_pad[...],
            (((1,), (1,)), ((), ())),
            precision=HIGH,
            preferred_element_type=F32,
        )
        own = [jnp.zeros((VEC, 64), F32) for _ in range(3 * OWNED)]
        for s in range(ENTRIES):
            mine = jnp.where(entry_of == s, cross[VEC * s : VEC * s + VEC, :], 0.0)
            for a in range(3 * OWNED):
                own[a] = own[a] + jnp.where(relative[s] == a, mine, 0.0)
        for a in range(3 * OWNED):
            coef_out[step, a, :, 0:64] = own[a]
        copies = [
            send(coef_out.at[step, 0:4], coef_p1.at[step], ring(-1)),
            send(coef_out.at[step, 2:6], coef_m1.at[step], ring(1)),
            send(coef_out.at[step, 0:2], coef_p2.at[step], ring(-2)),
            send(coef_out.at[step, 4:6], coef_m2.at[step], ring(2)),
        ]
        return copies

    def coef_finish(step, copies):
        for copy in copies:
            copy.wait()
        own = coef_out[step, :, :, 0:64]
        left2, left1 = coef_m2[step, :, :, 0:64], coef_m1[step, :, :, 0:64]
        right1, right2 = coef_p1[step, :, :, 0:64], coef_p2[step, :, :, 0:64]
        total = [
            own[0] + left1[0] + left2[0],
            own[1] + left1[1] + left2[1],
            own[2] + left1[2] + right1[0],
            own[3] + left1[3] + right1[1],
            own[4] + right1[2] + right2[0],
            own[5] + right1[3] + right2[1],
        ]
        stacked = jnp.concatenate(total, axis=0)
        coef = jnp.dot(stacked, fold, precision=HIGH, preferred_element_type=F32)
        coef = jnp.where(same_atom, coef, 0.0)
        return jnp.dot(coef, atom_tiled, precision=HIGH, preferred_element_type=F32)

    def own_energy(step, copies):
        for copy in copies:
            copy.wait()
        total = jnp.concatenate(
            [
                coef_out[step, OWNED + a, :, 0:64]
                + coef_m1[step, OWNED + a, :, 0:64]
                + coef_p1[step, a, :, 0:64]
                for a in range(OWNED)
            ],
            axis=0,
        )
        coef = jnp.dot(total, fold[:, 0:16], precision=HIGH, preferred_element_type=F32)
        coef = jnp.where(same_atom[0:16, 0:16], coef, 0.0)
        term = jnp.dot(
            coef, atom_tiled[16:32, :], precision=HIGH, preferred_element_type=F32
        )
        both = total * term
        return jnp.sum(both[0:VEC] + both[VEC : 2 * VEC], axis=1, keepdims=True)

    def support_products(term):
        chosen = jnp.zeros((VEC, 64), F32)
        for a in range(3 * OWNED):
            chosen = chosen + jnp.where(atom_row == a, term[VEC * a : VEC * a + VEC, :], 0.0)
        back = jnp.concatenate(
            [jnp.where(entry_of == s, chosen, 0.0) for s in range(ENTRIES)], axis=0
        )
        out = jnp.dot(back, proj_pad[...], precision=HIGH, preferred_element_type=F32)
        for s in range(ENTRIES):
            up, down = split(out[VEC * s : VEC * s + VEC, :])
            packed[CELLS + s] = jnp.concatenate([up, down], axis=0)

    def cell_products():
        uh = lhs_hi[...].reshape(CELLS * VEC, PAD)
        ul = lhs_lo[...].reshape(CELLS * VEC, PAD)
        out = jnp.dot(uh, stiff_hi[...], preferred_element_type=F32)
        out = out + jnp.dot(uh, stiff_lo[...], preferred_element_type=F32)
        out = out + jnp.dot(ul, stiff_hi[...], preferred_element_type=F32)
        energy = jnp.zeros((VEC, PAD), F32)
        for c in range(CELLS):
            full = out[VEC * c : VEC * c + VEC, :]
            up, down = split(full)
            packed[c] = jnp.concatenate([up, down], axis=0)
            energy = energy + full * values[c]
        return energy

    def assembled(k):
        both = acc[16 * k : 16 * k + 8, :] + acc[16 * k + 8 : 16 * k + 16, :]
        if EDGE <= k < EDGE + OWN:
            extra = []
            for t in range(2):
                diagonal = row(pot_ref, 2 * (k - EDGE) + t) + shift_col
                extra.append(diagonal * win[k, :, 128 * t : 128 * t + 128])
            both = both + jnp.concatenate(extra, axis=1)
        return both

    prepare_rim(ghost_blocks)
    gather_rim(ghost_blocks, PAIRS, SLOT_PAIRS, False)
    coefs = coef_start(0)
    gather_rim(ghost_blocks, 0, PAIRS, True)
    cell_products()
    acc[...] = jnp.zeros_like(acc)
    scatter(0, PAIRS)
    term = coef_finish(0, coefs)
    support_products(term)
    scatter(PAIRS, SLOT_PAIRS)
    for k in rim_blocks:
        v_one[k] = assembled(k)
    rims = [
        send(v_one.at[0 : 2 * EDGE], rim_right.at[0], ring(-1)),
        send(v_one.at[OWN:ROWS], rim_left.at[0], ring(1)),
    ]
    for k in inner_blocks:
        v_one[k] = assembled(k)

    sums = [jnp.zeros((VEC, 128), F32) for _ in range(3)]

    def advance(k, sums):
        a_acc, c_acc, d_acc = sums
        for t in range(2):
            at = slice(128 * t, 128 * t + 128)
            index = 2 * (k - EDGE) + t
            image = v_one[k, :, at]
            a_acc = a_acc + image * win[k, :, at]
            w = image * row(pre_ref, index)
            win[k, :, at] = w
            c_acc = c_acc + image * w
            d_acc = d_acc + (row(pot_ref, index) + shift_col) * w * w
        return [a_acc, c_acc, d_acc]

    for k in inner_blocks:
        sums = advance(k, sums)
    gather_main(inner_blocks)
    for copy in rims:
        copy.wait()
    for k in range(2 * EDGE):
        v_one[k] = v_one[k] + jnp.where(not_first, rim_left[0, k], 0.0)
        v_one[OWN + k] = v_one[OWN + k] + jnp.where(not_last, rim_right[0, k], 0.0)
    for k in rim_blocks:
        if EDGE <= k < EDGE + OWN:
            sums = advance(k, sums)
    for k in range(EDGE):
        for t in range(2):
            at = slice(128 * t, 128 * t + 128)
            left = row(pre_in.at[0], 2 * k + t) * v_one[k, :, at]
            win[k, :, at] = jnp.where(not_first, left, 0.0)
            right = row(pre_in.at[1], 2 * k + t) * v_one[OWN + EDGE + k, :, at]
            win[OWN + EDGE + k, :, at] = jnp.where(not_last, right, 0.0)

    prepare_rim(rim_blocks)
    gather_rim(rim_blocks, PAIRS, SLOT_PAIRS, False)
    coefs = coef_start(1)
    gather_rim(rim_blocks, 0, PAIRS, True)
    energy = cell_products()
    acc[...] = jnp.zeros_like(acc)
    scatter(0, 4)
    support_energy = own_energy(1, coefs[0:2])

    a_acc, c_acc, d_acc = sums
    for t in range(3):
        d_acc = d_acc + energy[:, 128 * t : 128 * t + 128]
    column = lax.broadcasted_iota(jnp.int32, (VEC, 128), 1)
    place = column - 4 * sublane
    tile = jnp.zeros((VEC, 128), F32)
    locals_ = (
        gamma,
        jnp.sum(a_acc, axis=1, keepdims=True),
        jnp.sum(c_acc, axis=1, keepdims=True),
        jnp.sum(d_acc, axis=1, keepdims=True) + support_energy,
    )
    for i, value in enumerate(locals_):
        tile = jnp.where(place == i, value, tile)
    tile = jnp.sum(tile, axis=0, keepdims=True)

    def reduce_start(stage, value):
        red_out[stage] = value
        return [
            send(red_out.at[stage], red_in.at[15 * stage + i], other)
            for i, other in enumerate(stages[stage])
        ]

    def reduce_finish(stage, copies, value):
        for copy in copies:
            copy.wait()
        for i in range(len(copies)):
            value = value + red_in[15 * stage + i]
        return value

    going = reduce_start(0, tile)
    scatter(4, PAIRS)
    term = coef_finish(1, coefs[2:4])
    support_products(term)
    scatter(PAIRS, SLOT_PAIRS)
    for k in rim_blocks:
        v_two[k] = assembled(k)
    rims = [
        send(v_two.at[0:EDGE], rim_right.at[1, 0:EDGE], ring(-1)),
        send(v_two.at[ROWS - EDGE : ROWS], rim_left.at[1, 0:EDGE], ring(1)),
    ]
    tile = reduce_finish(0, going, tile)
    going = reduce_start(1, tile)
    for k in inner_blocks:
        v_two[k] = assembled(k)
    for copy in rims:
        copy.wait()
    for k in range(EDGE):
        v_two[EDGE + k] = v_two[EDGE + k] + jnp.where(not_first, rim_left[1, k], 0.0)
        v_two[OWN + k] = v_two[OWN + k] + jnp.where(not_last, rim_right[1, k], 0.0)
    tile = reduce_finish(1, going, tile)
    gamma, a_sum, c_sum, d_sum = [
        jnp.sum(jnp.where(place == i, jnp.broadcast_to(tile, (VEC, 128)), 0.0), axis=1, keepdims=True)
        for i in range(4)
    ]
    step_one = gamma / a_sum
    fresh = gamma - 2.0 * step_one * a_sum + step_one * step_one * c_sum
    grow = 1.0 + fresh / gamma
    curve = grow * grow * a_sum - 2.0 * grow * step_one * c_sum + step_one * step_one * d_sum
    step_two = fresh / curve
    along = jnp.broadcast_to(step_one + step_two * grow, (VEC, LANES))
    across = jnp.broadcast_to(step_one * step_two, (VEC, LANES))
    for k in range(OWN):
        r = rhs_ref[:, LANES * k : LANES * k + LANES]
        image = v_one[EDGE + k]
        sol_ref[k] = along * (r * wide_row(pre_ref, k)) - across * win[EDGE + k]
        res_ref[k] = r - along * image + across * v_two[EDGE + k]


PARTS = 2


def hand_over(answer_ref, left_ref, answer_out, left_out, held, load_sem, store_sem):
    size = OWN // PARTS
    loads, stores = [], []
    for i, (src, dst) in enumerate(((answer_ref, answer_out), (left_ref, left_out))):
        for p in range(PARTS):
            piece = pl.ds(size * p, size)
            at = PARTS * i + p
            load = pltpu.make_async_copy(src.at[piece], held.at[i, piece], load_sem.at[at])
            load.start()
            loads.append(load)
            stores.append(
                pltpu.make_async_copy(held.at[i, piece], dst.at[piece], store_sem.at[at])
            )
    for load, store in zip(loads, stores):
        load.wait()
        store.start()
    for store in stores:
        store.wait()


SENDS = 6 + 2 * 4 + 2 * 2 + 30


def on_device(
    rhs,
    potential,
    precond,
    shift,
    stiffness,
    cell_scale,
    conn,
    cell_count,
    projector,
    support_cell,
    support_atom,
    support_count,
    atom_matrix,
):
    vmem = pl.BlockSpec(memory_space=pltpu.VMEM)
    smem = pl.BlockSpec(memory_space=pltpu.SMEM)
    field = jax.ShapeDtypeStruct((OWN, VEC, LANES), F32)
    anywhere = pl.BlockSpec(memory_space=pl.ANY)
    answer, left = pl.pallas_call(
        kernel,
        name="pcg",
        out_shape=(field, field),
        in_specs=[smem] * 6 + [anywhere] * 7,
        out_specs=(vmem, vmem),
        scratch_shapes=[
            pltpu.VMEM((VEC, NODE_DEV), F32),
            pltpu.VMEM((52, 128), F32),
            pltpu.VMEM((52, 128), F32),
            pltpu.VMEM((ELEM, ELEM), F32),
            pltpu.VMEM((CELLS, ELEM), jnp.int32),
            pltpu.VMEM((ENTRIES * NPROJ, ELEM), F32),
            pltpu.VMEM((OWNED * NPROJ, NPROJ), F32),
            pltpu.VMEM((ROWS, VEC, LANES), F32),
            pltpu.VMEM((2, ROWS * VEC, LANES), BF16),
            pltpu.VMEM((4 * EDGE * VEC * 2, LANES), BF16),
            pltpu.VMEM((SLOT_PAIRS, LANES, 2 * PAD), BF16),
            pltpu.VMEM((SLOTS, 1, PAD), jnp.int32),
            pltpu.VMEM((SLOTS, 1, PAD), jnp.int32),
            pltpu.VMEM((SLOTS, 16, PAD), jnp.int16),
            pltpu.VMEM((SLOTS, VEC, PAD), F32),
            pltpu.VMEM((PAIRS, 16, PAD), BF16),
            pltpu.VMEM((PAIRS, 16, PAD), BF16),
            pltpu.VMEM((PAD, PAD), BF16),
            pltpu.VMEM((PAD, PAD), BF16),
            pltpu.VMEM((ENTRIES * NPROJ, PAD), F32),
            pltpu.VMEM((CELLS, PAD), jnp.int32),
            pltpu.VMEM((SLOTS, 16, PAD), BF16),
            pltpu.VMEM((ROWS * 16, LANES), F32),
            pltpu.VMEM((ROWS, VEC, LANES), F32),
            pltpu.VMEM((ROWS, VEC, LANES), F32),
            pltpu.VMEM((2, 2 * EDGE, VEC, LANES), F32),
            pltpu.VMEM((2, 2 * EDGE, VEC, LANES), F32),
            pltpu.VMEM((2, 8, 128), F32),
            pltpu.VMEM((2, 8, 128), F32),
            pltpu.VMEM((2, OWNED * NPROJ, NPROJ), F32),
            pltpu.VMEM((2, 3 * OWNED, VEC, 128), F32),
            pltpu.VMEM((2, 2, VEC, 128), F32),
            pltpu.VMEM((2, 4, VEC, 128), F32),
            pltpu.VMEM((2, 4, VEC, 128), F32),
            pltpu.VMEM((2, 2, VEC, 128), F32),
            pltpu.VMEM((2, 1, 128), F32),
            pltpu.VMEM((30, 1, 128), F32),
            pltpu.SemaphoreType.DMA((7,)),
            pltpu.SemaphoreType.DMA((SENDS,)),
            pltpu.SemaphoreType.DMA((SENDS,)),
        ],
        compiler_params=pltpu.CompilerParams(
            collective_id=0, has_side_effects=True, vmem_limit_bytes=60 << 20
        ),
    )(
        cell_count,
        support_cell,
        support_atom,
        support_count,
        shift,
        cell_scale,
        rhs,
        potential.reshape(52, 128),
        precond.reshape(52, 128),
        stiffness,
        conn,
        projector.reshape(ENTRIES * NPROJ, ELEM),
        atom_matrix.reshape(OWNED * NPROJ, NPROJ),
    )

    answer, left = pl.pallas_call(
        hand_over,
        name="hand_over",
        out_shape=(field, field),
        in_specs=[anywhere] * 2,
        out_specs=(anywhere, anywhere),
        scratch_shapes=[
            pltpu.VMEM((2, OWN, VEC, LANES), F32),
            pltpu.SemaphoreType.DMA((2 * PARTS,)),
            pltpu.SemaphoreType.DMA((2 * PARTS,)),
        ],
        compiler_params=pltpu.CompilerParams(vmem_limit_bytes=60 << 20),
    )(answer, left)

    def rows(blocks):
        return jnp.transpose(blocks, (1, 0, 2)).reshape(VEC, NODE_DEV)

    return (rows(answer), rows(left))


def solution(mesh):
    in_specs = (
        P(None, "dom"),
        P("dom"),
        P("dom"),
        P(),
        P(),
        P("dom"),
        P("dom", None),
        P(),
        P("dom", None, None),
        P("dom"),
        P("dom"),
        P(),
        P("dom", None, None),
    )
    out_specs = (P(None, "dom"), P(None, "dom"))
    return jax.shard_map(
        on_device, mesh=mesh, in_specs=in_specs, out_specs=out_specs, check_vma=False
    )
```

```python
import jax
import jax.numpy as jnp
from jax import lax
from jax.experimental import pallas as pl
from jax.experimental.pallas import tpu as pltpu
from jax.sharding import PartitionSpec as P

F32 = jnp.float32
BF16 = jnp.bfloat16
HIGH = lax.Precision.HIGHEST
MESH = pl.DeviceIdType.MESH

VEC = 8
NPROJ = 8
ELEM = 343
PAD = 384
CELLS = 32
PAIRS = CELLS // 2
ENTRIES = 8
SLOTS = CELLS + ENTRIES
SLOT_PAIRS = SLOTS // 2
OWNED = 2
NODE_DEV = 6656
GHOST = 416
LANES = 256
OWN = NODE_DEV // LANES
EDGE = 2
ROWS = OWN + 2 * EDGE
SHIFT = EDGE * LANES - GHOST
N_DOM = 256


def kernel(
    count_ref,
    support_cell_ref,
    support_atom_ref,
    support_count_ref,
    shift_ref,
    scale_ref,
    rhs_hbm,
    pot_hbm,
    pre_hbm,
    stiff_hbm,
    conn_hbm,
    proj_hbm,
    atom_hbm,
    sol_ref,
    res_ref,
    rhs_ref,
    pot_ref,
    pre_ref,
    stiff_ref,
    conn_ref,
    proj_ref,
    atom_ref,
    win,
    split_main,
    split_rim,
    onehot,
    pos_ref,
    hi_ref,
    hi_wide,
    values,
    lhs_hi,
    lhs_lo,
    stiff_hi,
    stiff_lo,
    proj_pad,
    spread_ref,
    packed,
    acc,
    v_one,
    v_two,
    rim_left,
    rim_right,
    pre_out,
    pre_in,
    atom_in,
    coef_out,
    coef_m2,
    coef_m1,
    coef_p1,
    coef_p2,
    red_out,
    red_in,
    load_sem,
    send_sem,
    recv_sem,
):
    me = lax.axis_index("dom")

    def ring(step):
        return lax.rem(me + (step + N_DOM), N_DOM)

    low16 = lax.rem(me, 16)
    high16 = lax.div(me, 16)
    stages = (
        [me - low16 + lax.rem(low16 + d, 16) for d in range(1, 16)],
        [low16 + 16 * lax.rem(high16 + d, 16) for d in range(1, 16)],
    )
    greeted = [ring(-2), ring(-1), ring(1), ring(2)]
    for group in stages:
        greeted = greeted + group
    barrier = pltpu.get_barrier_semaphore()
    for other in greeted[0:4]:
        pl.semaphore_signal(barrier, inc=1, device_id=(other,), device_id_type=MESH)

    loads = []
    for i, (src, dst) in enumerate(
        (
            (conn_hbm, conn_ref),
            (rhs_hbm, rhs_ref),
            (pre_hbm, pre_ref),
            (atom_hbm, atom_ref),
            (proj_hbm, proj_ref),
            (stiff_hbm, stiff_ref),
            (pot_hbm, pot_ref),
        )
    ):
        load = pltpu.make_async_copy(src, dst, load_sem.at[i])
        load.start()
        loads.append(load)

    for other in greeted[4:]:
        pl.semaphore_signal(barrier, inc=1, device_id=(other,), device_id_type=MESH)

    used = [0]

    def send(src, dst, target):
        slot = used[0]
        used[0] = slot + 1
        copy = pltpu.make_async_remote_copy(
            src_ref=src,
            dst_ref=dst,
            send_sem=send_sem.at[slot],
            recv_sem=recv_sem.at[slot],
            device_id=(target,),
            device_id_type=MESH,
        )
        copy.start()
        return copy

    def row(ref, index):
        return jnp.broadcast_to(ref[index : index + 1, :], (VEC, 128))

    def wide_row(ref, k):
        return jnp.concatenate([row(ref, 2 * k), row(ref, 2 * k + 1)], axis=1)

    for load in loads[1:4]:
        load.wait()
    dot_acc = jnp.zeros((VEC, 128), F32)
    for k in range(OWN):
        for t in range(2):
            column = LANES * k + 128 * t
            r = rhs_ref[:, column : column + 128]
            p = r * row(pre_ref, 2 * k + t)
            win[EDGE + k, :, 128 * t : 128 * t + 128] = p
            dot_acc = dot_acc + r * p
    gamma = jnp.sum(dot_acc, axis=1, keepdims=True)
    pre_out[...] = jnp.zeros_like(pre_out)
    pre_out[0, 0:4, :] = pre_ref[0:4, :]
    pre_out[1, 0:4, :] = pre_ref[48:52, :]
    pl.semaphore_wait(barrier, len(greeted))
    first = [
        send(win.at[EDGE : 2 * EDGE], win.at[ROWS - EDGE : ROWS], ring(-1)),
        send(win.at[OWN : OWN + EDGE], win.at[0:EDGE], ring(1)),
        send(pre_out.at[0], pre_in.at[1], ring(-1)),
        send(pre_out.at[1], pre_in.at[0], ring(1)),
        send(atom_ref, atom_in.at[1], ring(-1)),
        send(atom_ref, atom_in.at[0], ring(1)),
    ]

    loads[0].wait()
    spread_ref[...] = jnp.full((CELLS, PAD), -1, jnp.int32)
    spread_ref[:, 0:ELEM] = conn_ref[...] + SHIFT
    for c in range(CELLS):
        pos_ref[c] = spread_ref[c : c + 1, :]
    for s in range(ENTRIES):
        pos_ref[CELLS + s] = pos_ref[support_cell_ref[s]]
    number = lax.broadcasted_iota(jnp.int32, (LANES, PAD), 0).astype(jnp.int16)

    def build(c, carry):
        for q in range(2):
            slot = 2 * c + q
            place = pos_ref[slot]
            high = jnp.right_shift(place, 8)
            hi_ref[slot] = high
            hi_wide[slot] = jnp.broadcast_to(high, (16, PAD)).astype(jnp.int16)
            low = jnp.bitwise_and(place, LANES - 1)
            low = jnp.broadcast_to(low, (16, PAD)).astype(jnp.int16)
            one = jnp.ones((16, PAD), BF16)
            zero = jnp.zeros((16, PAD), BF16)
            for r in range(LANES // 16):
                hit = jnp.where(number[16 * r : 16 * r + 16, :] == low, one, zero)
                onehot[c, 16 * r : 16 * r + 16, PAD * q : PAD * q + PAD] = hit
        return carry

    lax.fori_loop(0, SLOT_PAIRS, build, 0)

    live_cells = count_ref[me]

    def split(block):
        up = block.astype(BF16)
        return up, (block - up.astype(F32)).astype(BF16)

    def gather_main(blocks):
        count = len(blocks) * VEC
        for i, k in enumerate(blocks):
            up, down = split(win[k])
            split_main[0, VEC * i : VEC * i + VEC, :] = up
            split_main[1, VEC * i : VEC * i + VEC, :] = down

        def body(c, carry):
            oh = onehot[c]
            g = jnp.dot(split_main[0, 0:count, :], oh, preferred_element_type=F32) + jnp.dot(
                split_main[1, 0:count, :], oh, preferred_element_type=F32
            )
            for q in range(2):
                for t in range(3):
                    h = jnp.broadcast_to(
                        hi_ref[2 * c + q, :, 128 * t : 128 * t + 128], (VEC, 128)
                    )
                    got = jnp.zeros((VEC, 128), F32)
                    at = PAD * q + 128 * t
                    for i, k in enumerate(blocks):
                        got = jnp.where(h == k, g[VEC * i : VEC * i + VEC, at : at + 128], got)
                    values[2 * c + q, :, 128 * t : 128 * t + 128] = got
            return carry

        lax.fori_loop(0, SLOT_PAIRS, body, 0, unroll=10)

    def prepare_rim(blocks):
        count = len(blocks) * VEC
        for i, k in enumerate(blocks):
            up, down = split(win[k])
            split_rim[VEC * i : VEC * i + VEC, :] = up
            split_rim[count + VEC * i : count + VEC * i + VEC, :] = down

    def gather_rim(blocks, first_pair, last_pair, cells):
        count = len(blocks) * VEC

        def body(c, carry):
            g = jnp.dot(split_rim[0 : 2 * count, :], onehot[c], preferred_element_type=F32)
            g = g[0:count] + g[count : 2 * count]
            ups, downs = [], []
            for q in range(2):
                slot = 2 * c + q
                parts = []
                for t in range(3):
                    h = jnp.broadcast_to(hi_ref[slot, :, 128 * t : 128 * t + 128], (VEC, 128))
                    got = values[slot, :, 128 * t : 128 * t + 128]
                    at = PAD * q + 128 * t
                    for i, k in enumerate(blocks):
                        got = jnp.where(h == k, g[VEC * i : VEC * i + VEC, at : at + 128], got)
                    parts.append(got)
                full = jnp.concatenate(parts, axis=1)
                values[slot] = full
                if cells:
                    weight = jnp.where(slot < live_cells, scale_ref[slot], 0.0)
                    up, down = split(full * weight)
                    ups.append(up)
                    downs.append(down)
            if cells:
                lhs_hi[c] = jnp.concatenate(ups, axis=0)
                lhs_lo[c] = jnp.concatenate(downs, axis=0)
            return carry

        lax.fori_loop(first_pair, last_pair, body, 0, unroll=last_pair - first_pair)

    def scatter(first_pair, last_pair):
        def body(c, carry):
            v = jnp.concatenate([packed[2 * c], packed[2 * c + 1]], axis=1)
            h = jnp.concatenate([hi_wide[2 * c], hi_wide[2 * c + 1]], axis=1)
            zero = jnp.zeros_like(v)
            a = jnp.concatenate([jnp.where(h == k, v, zero) for k in range(ROWS)], axis=0)
            acc[...] += lax.dot_general(
                a, onehot[c], (((1,), (1,)), ((), ())), preferred_element_type=F32
            )
            return carry

        lax.fori_loop(first_pair, last_pair, body, 0, unroll=last_pair - first_pair)

    own_blocks = list(range(EDGE, EDGE + OWN))
    ghost_blocks = list(range(EDGE)) + list(range(EDGE + OWN, ROWS))
    inner_blocks = list(range(2 * EDGE, OWN))
    rim_blocks = list(range(2 * EDGE)) + list(range(OWN, ROWS))

    gather_main(own_blocks)

    for load in loads[4:]:
        load.wait()
    stiff_hi[...] = jnp.zeros_like(stiff_hi)
    stiff_lo[...] = jnp.zeros_like(stiff_lo)
    up, down = split(stiff_ref[...])
    stiff_hi[0:ELEM, 0:ELEM] = up
    stiff_lo[0:ELEM, 0:ELEM] = down
    proj_pad[...] = jnp.zeros_like(proj_pad)
    proj_pad[:, 0:ELEM] = proj_ref[...]

    lane64 = lax.broadcasted_iota(jnp.int32, (1, 64), 1)
    entry_of = jnp.right_shift(lane64, 3)
    channel_of = jnp.bitwise_and(lane64, 7)
    live_entries = support_count_ref[me]
    atom_row = jnp.full((1, 64), -1, jnp.int32)
    relative = []
    for s in range(ENTRIES):
        own_atom = jnp.where(s < live_entries, support_atom_ref[s] - (me - 1) * OWNED, -1)
        relative.append(own_atom)
        atom_row = jnp.where(entry_of == s, own_atom, atom_row)
    sublane = lax.broadcasted_iota(jnp.int32, (VEC, 128), 0)
    shift_col = jnp.zeros((VEC, 128), F32)
    for v in range(VEC):
        shift_col = jnp.where(sublane == v, shift_ref[v], shift_col)
    r48 = lax.broadcasted_iota(jnp.int32, (48, 48), 0)
    d48 = lax.broadcasted_iota(jnp.int32, (48, 48), 1)
    same_atom = jnp.right_shift(r48, 3) == jnp.right_shift(d48, 3)
    r8 = lax.broadcasted_iota(jnp.int32, (8, 64), 0)
    c64 = lax.broadcasted_iota(jnp.int32, (8, 64), 1)
    tile8 = jnp.where(r8 == jnp.bitwise_and(c64, 7), 1.0, 0.0).astype(F32)
    for copy in first:
        copy.wait()
    not_first = me > 0
    not_last = me < N_DOM - 1
    for k in range(EDGE):
        win[k] = jnp.where(not_first, win[k], 0.0)
        win[ROWS - EDGE + k] = jnp.where(not_last, win[ROWS - EDGE + k], 0.0)
    atoms = jnp.concatenate([atom_in[0], atom_ref[...], atom_in[1]], axis=0)
    atom_tiled = jnp.dot(atoms, tile8, precision=HIGH, preferred_element_type=F32)

    def coef_start(step):
        own = [jnp.zeros((VEC, 64), F32) for _ in range(3 * OWNED)]
        for s in range(ENTRIES):
            field = values[CELLS + s]
            mine = jnp.zeros((VEC, 64), F32)
            for j in range(NPROJ):
                at = NPROJ * s + j
                sums = jnp.sum(field * proj_pad[at : at + 1, :], axis=1, keepdims=True)
                mine = jnp.where(channel_of == j, sums, mine)
            for a in range(3 * OWNED):
                own[a] = own[a] + jnp.where(relative[s] == a, mine, 0.0)
        for a in range(3 * OWNED):
            coef_out[step, a, :, 0:64] = own[a]
        copies = [
            send(coef_out.at[step, 0:4], coef_p1.at[step], ring(-1)),
            send(coef_out.at[step, 2:6], coef_m1.at[step], ring(1)),
            send(coef_out.at[step, 0:2], coef_p2.at[step], ring(-2)),
            send(coef_out.at[step, 4:6], coef_m2.at[step], ring(2)),
        ]
        return copies

    def coef_finish(step, copies):
        for copy in copies:
            copy.wait()
        own = coef_out[step, :, :, 0:64]
        left2, left1 = coef_m2[step, :, :, 0:64], coef_m1[step, :, :, 0:64]
        right1, right2 = coef_p1[step, :, :, 0:64], coef_p2[step, :, :, 0:64]
        total = [
            own[0] + left1[0] + left2[0],
            own[1] + left1[1] + left2[1],
            own[2] + left1[2] + right1[0],
            own[3] + left1[3] + right1[1],
            own[4] + right1[2] + right2[0],
            own[5] + right1[3] + right2[1],
        ]
        stacked = jnp.concatenate(total, axis=0)
        coef = jnp.where(same_atom, stacked[:, 0:48], 0.0)
        return jnp.dot(coef, atom_tiled, precision=HIGH, preferred_element_type=F32)

    def own_energy(step, copies):
        for copy in copies:
            copy.wait()
        total = jnp.concatenate(
            [
                coef_out[step, OWNED + a, :, 0:64]
                + coef_m1[step, OWNED + a, :, 0:64]
                + coef_p1[step, a, :, 0:64]
                for a in range(OWNED)
            ],
            axis=0,
        )
        coef = jnp.where(same_atom[0:16, 0:16], total[:, 0:16], 0.0)
        term = jnp.dot(
            coef, atom_tiled[16:32, :], precision=HIGH, preferred_element_type=F32
        )
        both = jnp.where(lane64 < NPROJ, total * term, 0.0)
        return jnp.sum(both[0:VEC] + both[VEC : 2 * VEC], axis=1, keepdims=True)

    def support_products(term):
        chosen = jnp.zeros((VEC, 64), F32)
        for a in range(3 * OWNED):
            chosen = chosen + jnp.where(atom_row == a, term[VEC * a : VEC * a + VEC, :], 0.0)
        back = jnp.concatenate(
            [jnp.where(entry_of == s, chosen, 0.0) for s in range(ENTRIES)], axis=0
        )
        out = jnp.dot(back, proj_pad[...], precision=HIGH, preferred_element_type=F32)
        for s in range(ENTRIES):
            up, down = split(out[VEC * s : VEC * s + VEC, :])
            packed[CELLS + s] = jnp.concatenate([up, down], axis=0)

    def cell_products():
        uh = lhs_hi[...].reshape(CELLS * VEC, PAD)
        ul = lhs_lo[...].reshape(CELLS * VEC, PAD)
        out = jnp.dot(uh, stiff_hi[...], preferred_element_type=F32)
        out = out + jnp.dot(uh, stiff_lo[...], preferred_element_type=F32)
        out = out + jnp.dot(ul, stiff_hi[...], preferred_element_type=F32)
        energy = jnp.zeros((VEC, PAD), F32)
        for c in range(CELLS):
            full = out[VEC * c : VEC * c + VEC, :]
            up, down = split(full)
            packed[c] = jnp.concatenate([up, down], axis=0)
            energy = energy + full * values[c]
        return energy

    def assembled(k):
        both = acc[16 * k : 16 * k + 8, :] + acc[16 * k + 8 : 16 * k + 16, :]
        if EDGE <= k < EDGE + OWN:
            extra = []
            for t in range(2):
                diagonal = row(pot_ref, 2 * (k - EDGE) + t) + shift_col
                extra.append(diagonal * win[k, :, 128 * t : 128 * t + 128])
            both = both + jnp.concatenate(extra, axis=1)
        return both

    prepare_rim(ghost_blocks)
    gather_rim(ghost_blocks, PAIRS, SLOT_PAIRS, False)
    coefs = coef_start(0)
    gather_rim(ghost_blocks, 0, PAIRS, True)
    cell_products()
    acc[...] = jnp.zeros_like(acc)
    scatter(0, PAIRS)
    term = coef_finish(0, coefs)
    support_products(term)
    scatter(PAIRS, SLOT_PAIRS)
    for k in rim_blocks:
        v_one[k] = assembled(k)
    rims = [
        send(v_one.at[0 : 2 * EDGE], rim_right.at[0], ring(-1)),
        send(v_one.at[OWN:ROWS], rim_left.at[0], ring(1)),
    ]
    for k in inner_blocks:
        v_one[k] = assembled(k)

    sums = [jnp.zeros((VEC, 128), F32) for _ in range(3)]

    def advance(k, sums):
        a_acc, c_acc, d_acc = sums
        for t in range(2):
            at = slice(128 * t, 128 * t + 128)
            index = 2 * (k - EDGE) + t
            image = v_one[k, :, at]
            a_acc = a_acc + image * win[k, :, at]
            w = image * row(pre_ref, index)
            win[k, :, at] = w
            c_acc = c_acc + image * w
            d_acc = d_acc + (row(pot_ref, index) + shift_col) * w * w
        return [a_acc, c_acc, d_acc]

    for k in inner_blocks:
        sums = advance(k, sums)
    gather_main(inner_blocks)
    for copy in rims:
        copy.wait()
    for k in range(2 * EDGE):
        v_one[k] = v_one[k] + jnp.where(not_first, rim_left[0, k], 0.0)
        v_one[OWN + k] = v_one[OWN + k] + jnp.where(not_last, rim_right[0, k], 0.0)
    for k in rim_blocks:
        if EDGE <= k < EDGE + OWN:
            sums = advance(k, sums)
    for k in range(EDGE):
        for t in range(2):
            at = slice(128 * t, 128 * t + 128)
            left = row(pre_in.at[0], 2 * k + t) * v_one[k, :, at]
            win[k, :, at] = jnp.where(not_first, left, 0.0)
            right = row(pre_in.at[1], 2 * k + t) * v_one[OWN + EDGE + k, :, at]
            win[OWN + EDGE + k, :, at] = jnp.where(not_last, right, 0.0)

    prepare_rim(rim_blocks)
    gather_rim(rim_blocks, PAIRS, SLOT_PAIRS, False)
    coefs = coef_start(1)
    gather_rim(rim_blocks, 0, PAIRS, True)
    energy = cell_products()
    acc[...] = jnp.zeros_like(acc)
    scatter(0, 4)
    support_energy = own_energy(1, coefs[0:2])

    a_acc, c_acc, d_acc = sums
    for t in range(3):
        d_acc = d_acc + energy[:, 128 * t : 128 * t + 128]
    column = lax.broadcasted_iota(jnp.int32, (VEC, 128), 1)
    place = column - 4 * sublane
    tile = jnp.zeros((VEC, 128), F32)
    locals_ = (
        gamma,
        jnp.sum(a_acc, axis=1, keepdims=True),
        jnp.sum(c_acc, axis=1, keepdims=True),
        jnp.sum(d_acc, axis=1, keepdims=True) + support_energy,
    )
    for i, value in enumerate(locals_):
        tile = jnp.where(place == i, value, tile)
    tile = jnp.sum(tile, axis=0, keepdims=True)

    def reduce_start(stage, value):
        red_out[stage] = value
        return [
            send(red_out.at[stage], red_in.at[15 * stage + i], other)
            for i, other in enumerate(stages[stage])
        ]

    def reduce_finish(stage, copies, value):
        for copy in copies:
            copy.wait()
        for i in range(len(copies)):
            value = value + red_in[15 * stage + i]
        return value

    going = reduce_start(0, tile)
    scatter(4, PAIRS)
    term = coef_finish(1, coefs[2:4])
    support_products(term)
    scatter(PAIRS, SLOT_PAIRS)
    for k in rim_blocks:
        v_two[k] = assembled(k)
    rims = [
        send(v_two.at[0:EDGE], rim_right.at[1, 0:EDGE], ring(-1)),
        send(v_two.at[ROWS - EDGE : ROWS], rim_left.at[1, 0:EDGE], ring(1)),
    ]
    tile = reduce_finish(0, going, tile)
    going = reduce_start(1, tile)
    for k in inner_blocks:
        v_two[k] = assembled(k)
    for copy in rims:
        copy.wait()
    for k in range(EDGE):
        v_two[EDGE + k] = v_two[EDGE + k] + jnp.where(not_first, rim_left[1, k], 0.0)
        v_two[OWN + k] = v_two[OWN + k] + jnp.where(not_last, rim_right[1, k], 0.0)
    tile = reduce_finish(1, going, tile)
    gamma, a_sum, c_sum, d_sum = [
        jnp.sum(jnp.where(place == i, jnp.broadcast_to(tile, (VEC, 128)), 0.0), axis=1, keepdims=True)
        for i in range(4)
    ]
    step_one = gamma / a_sum
    fresh = gamma - 2.0 * step_one * a_sum + step_one * step_one * c_sum
    grow = 1.0 + fresh / gamma
    curve = grow * grow * a_sum - 2.0 * grow * step_one * c_sum + step_one * step_one * d_sum
    step_two = fresh / curve
    along = jnp.broadcast_to(step_one + step_two * grow, (VEC, LANES))
    across = jnp.broadcast_to(step_one * step_two, (VEC, LANES))
    for k in range(OWN):
        r = rhs_ref[:, LANES * k : LANES * k + LANES]
        image = v_one[EDGE + k]
        sol_ref[k] = along * (r * wide_row(pre_ref, k)) - across * win[EDGE + k]
        res_ref[k] = r - along * image + across * v_two[EDGE + k]


PARTS = 2


def hand_over(answer_ref, left_ref, answer_out, left_out, sem):
    copies = []
    size = OWN // PARTS
    for i, (src, dst) in enumerate(((answer_ref, answer_out), (left_ref, left_out))):
        for p in range(PARTS):
            piece = pl.ds(size * p, size)
            copy = pltpu.make_async_copy(src.at[piece], dst.at[piece], sem.at[PARTS * i + p])
            copy.start()
            copies.append(copy)
    for copy in copies:
        copy.wait()


SENDS = 6 + 2 * 4 + 2 * 2 + 30


def on_device(
    rhs,
    potential,
    precond,
    shift,
    stiffness,
    cell_scale,
    conn,
    cell_count,
    projector,
    support_cell,
    support_atom,
    support_count,
    atom_matrix,
):
    vmem = pl.BlockSpec(memory_space=pltpu.VMEM)
    smem = pl.BlockSpec(memory_space=pltpu.SMEM)
    field = jax.ShapeDtypeStruct((OWN, VEC, LANES), F32)
    anywhere = pl.BlockSpec(memory_space=pl.ANY)
    answer, left = pl.pallas_call(
        kernel,
        name="pcg",
        out_shape=(field, field),
        in_specs=[smem] * 6 + [anywhere] * 7,
        out_specs=(vmem, vmem),
        scratch_shapes=[
            pltpu.VMEM((VEC, NODE_DEV), F32),
            pltpu.VMEM((52, 128), F32),
            pltpu.VMEM((52, 128), F32),
            pltpu.VMEM((ELEM, ELEM), F32),
            pltpu.VMEM((CELLS, ELEM), jnp.int32),
            pltpu.VMEM((ENTRIES * NPROJ, ELEM), F32),
            pltpu.VMEM((OWNED * NPROJ, NPROJ), F32),
            pltpu.VMEM((ROWS, VEC, LANES), F32),
            pltpu.VMEM((2, ROWS * VEC, LANES), BF16),
            pltpu.VMEM((4 * EDGE * VEC * 2, LANES), BF16),
            pltpu.VMEM((SLOT_PAIRS, LANES, 2 * PAD), BF16),
            pltpu.VMEM((SLOTS, 1, PAD), jnp.int32),
            pltpu.VMEM((SLOTS, 1, PAD), jnp.int32),
            pltpu.VMEM((SLOTS, 16, PAD), jnp.int16),
            pltpu.VMEM((SLOTS, VEC, PAD), F32),
            pltpu.VMEM((PAIRS, 16, PAD), BF16),
            pltpu.VMEM((PAIRS, 16, PAD), BF16),
            pltpu.VMEM((PAD, PAD), BF16),
            pltpu.VMEM((PAD, PAD), BF16),
            pltpu.VMEM((ENTRIES * NPROJ, PAD), F32),
            pltpu.VMEM((CELLS, PAD), jnp.int32),
            pltpu.VMEM((SLOTS, 16, PAD), BF16),
            pltpu.VMEM((ROWS * 16, LANES), F32),
            pltpu.VMEM((ROWS, VEC, LANES), F32),
            pltpu.VMEM((ROWS, VEC, LANES), F32),
            pltpu.VMEM((2, 2 * EDGE, VEC, LANES), F32),
            pltpu.VMEM((2, 2 * EDGE, VEC, LANES), F32),
            pltpu.VMEM((2, 8, 128), F32),
            pltpu.VMEM((2, 8, 128), F32),
            pltpu.VMEM((2, OWNED * NPROJ, NPROJ), F32),
            pltpu.VMEM((2, 3 * OWNED, VEC, 128), F32),
            pltpu.VMEM((2, 2, VEC, 128), F32),
            pltpu.VMEM((2, 4, VEC, 128), F32),
            pltpu.VMEM((2, 4, VEC, 128), F32),
            pltpu.VMEM((2, 2, VEC, 128), F32),
            pltpu.VMEM((2, 1, 128), F32),
            pltpu.VMEM((30, 1, 128), F32),
            pltpu.SemaphoreType.DMA((7,)),
            pltpu.SemaphoreType.DMA((SENDS,)),
            pltpu.SemaphoreType.DMA((SENDS,)),
        ],
        compiler_params=pltpu.CompilerParams(
            collective_id=0, has_side_effects=True, vmem_limit_bytes=40 << 20
        ),
    )(
        pltpu.with_memory_space_constraint(cell_count, pltpu.HBM),
        pltpu.with_memory_space_constraint(support_cell, pltpu.HBM),
        pltpu.with_memory_space_constraint(support_atom, pltpu.HBM),
        pltpu.with_memory_space_constraint(support_count, pltpu.HBM),
        pltpu.with_memory_space_constraint(shift, pltpu.HBM),
        pltpu.with_memory_space_constraint(cell_scale, pltpu.HBM),
        pltpu.with_memory_space_constraint(rhs, pltpu.HBM),
        pltpu.with_memory_space_constraint(potential.reshape(52, 128), pltpu.HBM),
        pltpu.with_memory_space_constraint(precond.reshape(52, 128), pltpu.HBM),
        pltpu.with_memory_space_constraint(stiffness, pltpu.HBM),
        pltpu.with_memory_space_constraint(conn, pltpu.HBM),
        pltpu.with_memory_space_constraint(projector.reshape(ENTRIES * NPROJ, ELEM), pltpu.HBM),
        pltpu.with_memory_space_constraint(atom_matrix.reshape(OWNED * NPROJ, NPROJ), pltpu.HBM),
    )

    answer, left = pl.pallas_call(
        hand_over,
        name="hand_over",
        out_shape=(field, field),
        in_specs=[vmem] * 2,
        out_specs=(anywhere, anywhere),
        scratch_shapes=[pltpu.SemaphoreType.DMA((2 * PARTS,))],
    )(
        pltpu.with_memory_space_constraint(answer, pltpu.VMEM),
        pltpu.with_memory_space_constraint(left, pltpu.VMEM),
    )

    def rows(blocks):
        return jnp.transpose(blocks, (1, 0, 2)).reshape(VEC, NODE_DEV)

    return (rows(answer), rows(left))


def solution(mesh):
    in_specs = (
        P(None, "dom"),
        P("dom"),
        P("dom"),
        P(),
        P(),
        P("dom"),
        P("dom", None),
        P(),
        P("dom", None, None),
        P("dom"),
        P("dom"),
        P(),
        P("dom", None, None),
    )
    out_specs = (P(None, "dom"), P(None, "dom"))
    return jax.shard_map(
        on_device, mesh=mesh, in_specs=in_specs, out_specs=out_specs, check_vma=False
    )
```

```python
import jax
import jax.numpy as jnp
from jax import lax
from jax.experimental import pallas as pl
from jax.experimental.pallas import tpu as pltpu
from jax.sharding import PartitionSpec as P

F32 = jnp.float32
BF16 = jnp.bfloat16
HIGH = lax.Precision.HIGHEST
MESH = pl.DeviceIdType.MESH

VEC = 8
NPROJ = 8
ELEM = 343
PAD = 384
CELLS = 32
PAIRS = CELLS // 2
ENTRIES = 8
SLOTS = CELLS + ENTRIES
SLOT_PAIRS = SLOTS // 2
OWNED = 2
NODE_DEV = 6656
GHOST = 416
LANES = 256
OWN = NODE_DEV // LANES
EDGE = 2
ROWS = OWN + 2 * EDGE
SHIFT = EDGE * LANES - GHOST
N_DOM = 256


def kernel(
    count_ref,
    support_cell_ref,
    support_atom_ref,
    support_count_ref,
    shift_ref,
    scale_ref,
    rhs_hbm,
    pot_hbm,
    pre_hbm,
    stiff_hbm,
    conn_hbm,
    proj_hbm,
    atom_hbm,
    sol_ref,
    res_ref,
    rhs_ref,
    pot_ref,
    pre_ref,
    stiff_ref,
    conn_ref,
    proj_ref,
    atom_ref,
    win,
    split_main,
    split_rim,
    onehot,
    pos_ref,
    hi_ref,
    hi_wide,
    values,
    lhs_hi,
    lhs_lo,
    stiff_hi,
    stiff_lo,
    proj_pad,
    spread_ref,
    packed,
    acc,
    v_one,
    v_two,
    rim_left,
    rim_right,
    pre_out,
    pre_in,
    atom_in,
    coef_out,
    coef_m2,
    coef_m1,
    coef_p1,
    coef_p2,
    red_out,
    red_in,
    load_sem,
    send_sem,
    recv_sem,
):
    me = lax.axis_index("dom")

    def ring(step):
        return lax.rem(me + (step + N_DOM), N_DOM)

    low16 = lax.rem(me, 16)
    high16 = lax.div(me, 16)
    stages = (
        [me - low16 + lax.rem(low16 + d, 16) for d in range(1, 16)],
        [low16 + 16 * lax.rem(high16 + d, 16) for d in range(1, 16)],
    )
    greeted = [ring(-2), ring(-1), ring(1), ring(2)]
    for group in stages:
        greeted = greeted + group
    barrier = pltpu.get_barrier_semaphore()
    for other in greeted[0:4]:
        pl.semaphore_signal(barrier, inc=1, device_id=(other,), device_id_type=MESH)

    loads = []
    for i, (src, dst) in enumerate(
        (
            (conn_hbm, conn_ref),
            (rhs_hbm, rhs_ref),
            (pre_hbm, pre_ref),
            (atom_hbm, atom_ref),
            (proj_hbm, proj_ref),
            (stiff_hbm, stiff_ref),
            (pot_hbm, pot_ref),
        )
    ):
        load = pltpu.make_async_copy(src, dst, load_sem.at[i])
        load.start()
        loads.append(load)

    for other in greeted[4:]:
        pl.semaphore_signal(barrier, inc=1, device_id=(other,), device_id_type=MESH)

    used = [0]

    def send(src, dst, target):
        slot = used[0]
        used[0] = slot + 1
        copy = pltpu.make_async_remote_copy(
            src_ref=src,
            dst_ref=dst,
            send_sem=send_sem.at[slot],
            recv_sem=recv_sem.at[slot],
            device_id=(target,),
            device_id_type=MESH,
        )
        copy.start()
        return copy

    class RingCopy:
        def __init__(self, src, dst, step):
            slot = used[0]
            used[0] = slot + 1
            self.copy = pltpu.make_async_remote_copy(
                src_ref=src,
                dst_ref=dst,
                send_sem=send_sem.at[slot],
                recv_sem=recv_sem.at[slot],
                device_id=(ring(step),),
                device_id_type=MESH,
            )
            self.sends = me >= -step if step < 0 else me < N_DOM - step
            self.receives = me < N_DOM + step if step < 0 else me >= step

            @pl.when(self.sends)
            def _():
                self.copy.start()

        def wait(self):
            @pl.when(self.sends)
            def _():
                self.copy.wait_send()

            @pl.when(self.receives)
            def _():
                self.copy.wait_recv()

    def row(ref, index):
        return jnp.broadcast_to(ref[index : index + 1, :], (VEC, 128))

    def wide_row(ref, k):
        return jnp.concatenate([row(ref, 2 * k), row(ref, 2 * k + 1)], axis=1)

    for load in loads[1:4]:
        load.wait()
    dot_acc = jnp.zeros((VEC, 128), F32)
    for k in range(OWN):
        for t in range(2):
            column = LANES * k + 128 * t
            r = rhs_ref[:, column : column + 128]
            p = r * row(pre_ref, 2 * k + t)
            win[EDGE + k, :, 128 * t : 128 * t + 128] = p
            dot_acc = dot_acc + r * p
    gamma = jnp.sum(dot_acc, axis=1, keepdims=True)
    pre_out[...] = jnp.zeros_like(pre_out)
    pre_out[0, 0:4, :] = pre_ref[0:4, :]
    pre_out[1, 0:4, :] = pre_ref[48:52, :]
    pl.semaphore_wait(barrier, len(greeted))
    first = [
        RingCopy(win.at[EDGE : 2 * EDGE], win.at[ROWS - EDGE : ROWS], -1),
        RingCopy(win.at[OWN : OWN + EDGE], win.at[0:EDGE], 1),
        RingCopy(pre_out.at[0], pre_in.at[1], -1),
        RingCopy(pre_out.at[1], pre_in.at[0], 1),
        RingCopy(atom_ref, atom_in.at[1], -1),
        RingCopy(atom_ref, atom_in.at[0], 1),
    ]

    loads[0].wait()
    spread_ref[...] = jnp.full((CELLS, PAD), -1, jnp.int32)
    spread_ref[:, 0:ELEM] = conn_ref[...] + SHIFT
    for c in range(CELLS):
        pos_ref[c] = spread_ref[c : c + 1, :]
    for s in range(ENTRIES):
        pos_ref[CELLS + s] = pos_ref[support_cell_ref[s]]
    number = lax.broadcasted_iota(jnp.int32, (LANES, PAD), 0).astype(jnp.int16)

    def build(c, carry):
        for q in range(2):
            slot = 2 * c + q
            place = pos_ref[slot]
            high = jnp.right_shift(place, 8)
            hi_ref[slot] = high
            hi_wide[slot] = jnp.broadcast_to(high, (16, PAD)).astype(jnp.int16)
            low = jnp.bitwise_and(place, LANES - 1)
            low = jnp.broadcast_to(low, (16, PAD)).astype(jnp.int16)
            one = jnp.ones((16, PAD), BF16)
            zero = jnp.zeros((16, PAD), BF16)
            for r in range(LANES // 16):
                hit = jnp.where(number[16 * r : 16 * r + 16, :] == low, one, zero)
                onehot[c, 16 * r : 16 * r + 16, PAD * q : PAD * q + PAD] = hit
        return carry

    lax.fori_loop(0, SLOT_PAIRS, build, 0)

    live_cells = count_ref[me]

    def split(block):
        up = block.astype(BF16)
        return up, (block - up.astype(F32)).astype(BF16)

    def gather_main(blocks):
        count = len(blocks) * VEC
        for i, k in enumerate(blocks):
            up, down = split(win[k])
            split_main[0, VEC * i : VEC * i + VEC, :] = up
            split_main[1, VEC * i : VEC * i + VEC, :] = down

        def body(c, carry):
            oh = onehot[c]
            g = jnp.dot(split_main[0, 0:count, :], oh, preferred_element_type=F32) + jnp.dot(
                split_main[1, 0:count, :], oh, preferred_element_type=F32
            )
            for q in range(2):
                for t in range(3):
                    h = jnp.broadcast_to(
                        hi_ref[2 * c + q, :, 128 * t : 128 * t + 128], (VEC, 128)
                    )
                    got = jnp.zeros((VEC, 128), F32)
                    at = PAD * q + 128 * t
                    for i, k in enumerate(blocks):
                        got = jnp.where(h == k, g[VEC * i : VEC * i + VEC, at : at + 128], got)
                    values[2 * c + q, :, 128 * t : 128 * t + 128] = got
            return carry

        lax.fori_loop(0, SLOT_PAIRS, body, 0, unroll=10)

    def prepare_rim(blocks):
        count = len(blocks) * VEC
        for i, k in enumerate(blocks):
            up, down = split(win[k])
            split_rim[VEC * i : VEC * i + VEC, :] = up
            split_rim[count + VEC * i : count + VEC * i + VEC, :] = down

    def gather_rim(blocks, first_pair, last_pair, cells):
        count = len(blocks) * VEC

        def body(c, carry):
            g = jnp.dot(split_rim[0 : 2 * count, :], onehot[c], preferred_element_type=F32)
            g = g[0:count] + g[count : 2 * count]
            ups, downs = [], []
            for q in range(2):
                slot = 2 * c + q
                parts = []
                for t in range(3):
                    h = jnp.broadcast_to(hi_ref[slot, :, 128 * t : 128 * t + 128], (VEC, 128))
                    got = values[slot, :, 128 * t : 128 * t + 128]
                    at = PAD * q + 128 * t
                    for i, k in enumerate(blocks):
                        got = jnp.where(h == k, g[VEC * i : VEC * i + VEC, at : at + 128], got)
                    parts.append(got)
                full = jnp.concatenate(parts, axis=1)
                values[slot] = full
                if cells:
                    weight = jnp.where(slot < live_cells, scale_ref[slot], 0.0)
                    up, down = split(full * weight)
                    ups.append(up)
                    downs.append(down)
            if cells:
                lhs_hi[c] = jnp.concatenate(ups, axis=0)
                lhs_lo[c] = jnp.concatenate(downs, axis=0)
            return carry

        lax.fori_loop(first_pair, last_pair, body, 0, unroll=last_pair - first_pair)

    def scatter(first_pair, last_pair):
        def body(c, carry):
            v = jnp.concatenate([packed[2 * c], packed[2 * c + 1]], axis=1)
            h = jnp.concatenate([hi_wide[2 * c], hi_wide[2 * c + 1]], axis=1)
            zero = jnp.zeros_like(v)
            a = jnp.concatenate([jnp.where(h == k, v, zero) for k in range(ROWS)], axis=0)
            acc[...] += lax.dot_general(
                a, onehot[c], (((1,), (1,)), ((), ())), preferred_element_type=F32
            )
            return carry

        lax.fori_loop(first_pair, last_pair, body, 0, unroll=last_pair - first_pair)

    own_blocks = list(range(EDGE, EDGE + OWN))
    ghost_blocks = list(range(EDGE)) + list(range(EDGE + OWN, ROWS))
    inner_blocks = list(range(2 * EDGE, OWN))
    rim_blocks = list(range(2 * EDGE)) + list(range(OWN, ROWS))

    gather_main(own_blocks)

    for load in loads[4:]:
        load.wait()
    stiff_hi[...] = jnp.zeros_like(stiff_hi)
    stiff_lo[...] = jnp.zeros_like(stiff_lo)
    up, down = split(stiff_ref[...])
    stiff_hi[0:ELEM, 0:ELEM] = up
    stiff_lo[0:ELEM, 0:ELEM] = down
    proj_pad[...] = jnp.zeros_like(proj_pad)
    proj_pad[:, 0:ELEM] = proj_ref[...]

    lane64 = lax.broadcasted_iota(jnp.int32, (1, 64), 1)
    entry_of = jnp.right_shift(lane64, 3)
    lane128 = lax.broadcasted_iota(jnp.int32, (1, 128), 1)
    channel_of = jnp.bitwise_and(lane128, 7)
    group_of = jnp.right_shift(lane128, 3)
    live_entries = support_count_ref[me]
    atom_row = jnp.full((1, 64), -1, jnp.int32)
    relative = []
    for s in range(ENTRIES):
        own_atom = jnp.where(s < live_entries, support_atom_ref[s] - (me - 1) * OWNED, -1)
        relative.append(own_atom)
        atom_row = jnp.where(entry_of == s, own_atom, atom_row)
    sublane = lax.broadcasted_iota(jnp.int32, (VEC, 128), 0)
    shift_col = jnp.zeros((VEC, 128), F32)
    for v in range(VEC):
        shift_col = jnp.where(sublane == v, shift_ref[v], shift_col)
    r8 = lax.broadcasted_iota(jnp.int32, (8, 64), 0)
    c64 = lax.broadcasted_iota(jnp.int32, (8, 64), 1)
    tile8 = jnp.where(r8 == jnp.bitwise_and(c64, 7), 1.0, 0.0).astype(F32)
    row_atom = jnp.right_shift(lax.broadcasted_iota(jnp.int32, (48, 64), 0), 3)
    column_atom = jnp.right_shift(lax.broadcasted_iota(jnp.int32, (48, 48), 1), 3)
    for copy in first:
        copy.wait()
    not_first = me > 0
    not_last = me < N_DOM - 1
    for k in range(EDGE):
        win[k] = jnp.where(not_first, win[k], 0.0)
        win[ROWS - EDGE + k] = jnp.where(not_last, win[ROWS - EDGE + k], 0.0)
    atoms_left = jnp.where(not_first, atom_in[0], 0.0)
    atoms_right = jnp.where(not_last, atom_in[1], 0.0)
    atoms = jnp.concatenate([atoms_left, atom_ref[...], atoms_right], axis=0)
    atom_tiled = jnp.dot(atoms, tile8, precision=HIGH, preferred_element_type=F32)
    entry_atoms = jnp.where(row_atom == atom_row, atom_tiled, 0.0)
    owned_column = (column_atom >= OWNED) & (column_atom < 2 * OWNED)
    diagonal_block = (row_atom[:, 0:48] == column_atom) & owned_column
    own_atoms = jnp.where(diagonal_block, atom_tiled[:, 0:48], 0.0)

    def coef_start(step):
        own = jnp.zeros((VEC, 128), F32)
        for s in range(ENTRIES):
            field = values[CELLS + s]
            mine = jnp.zeros((VEC, 128), F32)
            for j in range(NPROJ):
                at = NPROJ * s + j
                sums = jnp.sum(field * proj_pad[at : at + 1, :], axis=1, keepdims=True)
                mine = jnp.where(channel_of == j, sums, mine)
            own = own + jnp.where(group_of == relative[s], mine, 0.0)
        coef_out[step] = own
        copies = [
            RingCopy(coef_out.at[step], coef_p1.at[step], -1),
            RingCopy(coef_out.at[step], coef_m1.at[step], 1),
            RingCopy(coef_out.at[step], coef_p2.at[step], -2),
            RingCopy(coef_out.at[step], coef_m2.at[step], 2),
        ]
        return copies

    def moved(tile, blocks):
        return pltpu.roll(tile, (128 - 16 * blocks) % 128, axis=1)

    def near_sum(step):
        left = jnp.where(not_first, coef_m1[step], 0.0)
        right = jnp.where(not_last, coef_p1[step], 0.0)
        return coef_out[step] + moved(left, 1) + moved(right, -1)

    def coef_finish(step, copies):
        for copy in copies:
            copy.wait()
        left = jnp.where(me > 1, coef_m2[step], 0.0)
        right = jnp.where(me < N_DOM - 2, coef_p2[step], 0.0)
        total = near_sum(step) + moved(left, 2) + moved(right, -2)
        return jnp.dot(total[:, 0:48], entry_atoms, precision=HIGH, preferred_element_type=F32)

    def own_energy(step, copies):
        for copy in copies:
            copy.wait()
        total = near_sum(step)[:, 0:48]
        applied = jnp.dot(total, own_atoms, precision=HIGH, preferred_element_type=F32)
        return jnp.sum(total * applied, axis=1, keepdims=True)

    def support_products(chosen):
        back = jnp.concatenate(
            [jnp.where(entry_of == s, chosen, 0.0) for s in range(ENTRIES)], axis=0
        )
        out = jnp.dot(back, proj_pad[...], precision=HIGH, preferred_element_type=F32)
        for s in range(ENTRIES):
            up, down = split(out[VEC * s : VEC * s + VEC, :])
            packed[CELLS + s] = jnp.concatenate([up, down], axis=0)

    def cell_products():
        uh = lhs_hi[...].reshape(CELLS * VEC, PAD)
        ul = lhs_lo[...].reshape(CELLS * VEC, PAD)
        out = jnp.dot(uh, stiff_hi[...], preferred_element_type=F32)
        out = out + jnp.dot(uh, stiff_lo[...], preferred_element_type=F32)
        out = out + jnp.dot(ul, stiff_hi[...], preferred_element_type=F32)
        energy = jnp.zeros((VEC, PAD), F32)
        for c in range(CELLS):
            full = out[VEC * c : VEC * c + VEC, :]
            up, down = split(full)
            packed[c] = jnp.concatenate([up, down], axis=0)
            energy = energy + full * values[c]
        return energy

    def assembled(k):
        both = acc[16 * k : 16 * k + 8, :] + acc[16 * k + 8 : 16 * k + 16, :]
        if EDGE <= k < EDGE + OWN:
            extra = []
            for t in range(2):
                diagonal = row(pot_ref, 2 * (k - EDGE) + t) + shift_col
                extra.append(diagonal * win[k, :, 128 * t : 128 * t + 128])
            both = both + jnp.concatenate(extra, axis=1)
        return both

    prepare_rim(ghost_blocks)
    gather_rim(ghost_blocks, PAIRS, SLOT_PAIRS, False)
    coefs = coef_start(0)
    gather_rim(ghost_blocks, 0, PAIRS, True)
    cell_products()
    acc[...] = jnp.zeros_like(acc)
    scatter(0, PAIRS)
    term = coef_finish(0, coefs)
    support_products(term)
    scatter(PAIRS, SLOT_PAIRS)
    for k in rim_blocks:
        v_one[k] = assembled(k)
    rims = [
        RingCopy(v_one.at[0 : 2 * EDGE], rim_right.at[0], -1),
        RingCopy(v_one.at[OWN:ROWS], rim_left.at[0], 1),
    ]
    for k in inner_blocks:
        v_one[k] = assembled(k)

    sums = [jnp.zeros((VEC, 128), F32) for _ in range(3)]

    def advance(k, sums):
        a_acc, c_acc, d_acc = sums
        for t in range(2):
            at = slice(128 * t, 128 * t + 128)
            index = 2 * (k - EDGE) + t
            image = v_one[k, :, at]
            a_acc = a_acc + image * win[k, :, at]
            w = image * row(pre_ref, index)
            win[k, :, at] = w
            c_acc = c_acc + image * w
            d_acc = d_acc + (row(pot_ref, index) + shift_col) * w * w
        return [a_acc, c_acc, d_acc]

    for k in inner_blocks:
        sums = advance(k, sums)
    gather_main(inner_blocks)
    for copy in rims:
        copy.wait()
    for k in range(2 * EDGE):
        v_one[k] = v_one[k] + jnp.where(not_first, rim_left[0, k], 0.0)
        v_one[OWN + k] = v_one[OWN + k] + jnp.where(not_last, rim_right[0, k], 0.0)
    for k in rim_blocks:
        if EDGE <= k < EDGE + OWN:
            sums = advance(k, sums)
    for k in range(EDGE):
        for t in range(2):
            at = slice(128 * t, 128 * t + 128)
            left = row(pre_in.at[0], 2 * k + t) * v_one[k, :, at]
            win[k, :, at] = jnp.where(not_first, left, 0.0)
            right = row(pre_in.at[1], 2 * k + t) * v_one[OWN + EDGE + k, :, at]
            win[OWN + EDGE + k, :, at] = jnp.where(not_last, right, 0.0)

    prepare_rim(rim_blocks)
    gather_rim(rim_blocks, PAIRS, SLOT_PAIRS, False)
    coefs = coef_start(1)
    gather_rim(rim_blocks, 0, PAIRS, True)
    energy = cell_products()
    acc[...] = jnp.zeros_like(acc)
    scatter(0, 8)
    support_energy = own_energy(1, coefs[0:2])

    a_acc, c_acc, d_acc = sums
    for t in range(3):
        d_acc = d_acc + energy[:, 128 * t : 128 * t + 128]
    column = lax.broadcasted_iota(jnp.int32, (VEC, 128), 1)
    place = column - 4 * sublane
    tile = jnp.zeros((VEC, 128), F32)
    locals_ = (
        gamma,
        jnp.sum(a_acc, axis=1, keepdims=True),
        jnp.sum(c_acc, axis=1, keepdims=True),
        jnp.sum(d_acc, axis=1, keepdims=True) + support_energy,
    )
    for i, value in enumerate(locals_):
        tile = jnp.where(place == i, value, tile)
    tile = jnp.sum(tile, axis=0, keepdims=True)

    def reduce_start(stage, value):
        red_out[stage] = value
        return [
            send(red_out.at[stage], red_in.at[15 * stage + i], other)
            for i, other in enumerate(stages[stage])
        ]

    def reduce_finish(stage, copies, value):
        for copy in copies:
            copy.wait()
        for i in range(len(copies)):
            value = value + red_in[15 * stage + i]
        return value

    going = reduce_start(0, tile)
    scatter(8, PAIRS)
    term = coef_finish(1, coefs[2:4])
    support_products(term)
    scatter(PAIRS, SLOT_PAIRS)
    for k in rim_blocks:
        v_two[k] = assembled(k)
    rims = [
        RingCopy(v_two.at[0:EDGE], rim_right.at[1, 0:EDGE], -1),
        RingCopy(v_two.at[ROWS - EDGE : ROWS], rim_left.at[1, 0:EDGE], 1),
    ]
    tile = reduce_finish(0, going, tile)
    going = reduce_start(1, tile)
    for k in inner_blocks:
        v_two[k] = assembled(k)
    for copy in rims:
        copy.wait()
    for k in range(EDGE):
        v_two[EDGE + k] = v_two[EDGE + k] + jnp.where(not_first, rim_left[1, k], 0.0)
        v_two[OWN + k] = v_two[OWN + k] + jnp.where(not_last, rim_right[1, k], 0.0)
    tile = reduce_finish(1, going, tile)
    gamma, a_sum, c_sum, d_sum = [
        jnp.sum(jnp.where(place == i, jnp.broadcast_to(tile, (VEC, 128)), 0.0), axis=1, keepdims=True)
        for i in range(4)
    ]
    step_one = gamma / a_sum
    fresh = gamma - 2.0 * step_one * a_sum + step_one * step_one * c_sum
    grow = 1.0 + fresh / gamma
    curve = grow * grow * a_sum - 2.0 * grow * step_one * c_sum + step_one * step_one * d_sum
    step_two = fresh / curve
    along = jnp.broadcast_to(step_one + step_two * grow, (VEC, LANES))
    across = jnp.broadcast_to(step_one * step_two, (VEC, LANES))
    for k in range(OWN):
        r = rhs_ref[:, LANES * k : LANES * k + LANES]
        image = v_one[EDGE + k]
        sol_ref[k] = along * (r * wide_row(pre_ref, k)) - across * win[EDGE + k]
        res_ref[k] = r - along * image + across * v_two[EDGE + k]


PARTS = 2


def hand_over(answer_ref, left_ref, answer_out, left_out, sem):
    copies = []
    size = OWN // PARTS
    for i, (src, dst) in enumerate(((answer_ref, answer_out), (left_ref, left_out))):
        for p in range(PARTS):
            piece = pl.ds(size * p, size)
            copy = pltpu.make_async_copy(src.at[piece], dst.at[piece], sem.at[PARTS * i + p])
            copy.start()
            copies.append(copy)
    for copy in copies:
        copy.wait()


SENDS = 6 + 2 * 4 + 2 * 2 + 30


def on_device(
    rhs,
    potential,
    precond,
    shift,
    stiffness,
    cell_scale,
    conn,
    cell_count,
    projector,
    support_cell,
    support_atom,
    support_count,
    atom_matrix,
):
    vmem = pl.BlockSpec(memory_space=pltpu.VMEM)
    smem = pl.BlockSpec(memory_space=pltpu.SMEM)
    field = jax.ShapeDtypeStruct((OWN, VEC, LANES), F32)
    anywhere = pl.BlockSpec(memory_space=pl.ANY)
    answer, left = pl.pallas_call(
        kernel,
        name="pcg",
        out_shape=(field, field),
        in_specs=[smem] * 6 + [anywhere] * 7,
        out_specs=(vmem, vmem),
        scratch_shapes=[
            pltpu.VMEM((VEC, NODE_DEV), F32),
            pltpu.VMEM((52, 128), F32),
            pltpu.VMEM((52, 128), F32),
            pltpu.VMEM((ELEM, ELEM), F32),
            pltpu.VMEM((CELLS, ELEM), jnp.int32),
            pltpu.VMEM((ENTRIES * NPROJ, ELEM), F32),
            pltpu.VMEM((OWNED * NPROJ, NPROJ), F32),
            pltpu.VMEM((ROWS, VEC, LANES), F32),
            pltpu.VMEM((2, ROWS * VEC, LANES), BF16),
            pltpu.VMEM((4 * EDGE * VEC * 2, LANES), BF16),
            pltpu.VMEM((SLOT_PAIRS, LANES, 2 * PAD), BF16),
            pltpu.VMEM((SLOTS, 1, PAD), jnp.int32),
            pltpu.VMEM((SLOTS, 1, PAD), jnp.int32),
            pltpu.VMEM((SLOTS, 16, PAD), jnp.int16),
            pltpu.VMEM((SLOTS, VEC, PAD), F32),
            pltpu.VMEM((PAIRS, 16, PAD), BF16),
            pltpu.VMEM((PAIRS, 16, PAD), BF16),
            pltpu.VMEM((PAD, PAD), BF16),
            pltpu.VMEM((PAD, PAD), BF16),
            pltpu.VMEM((ENTRIES * NPROJ, PAD), F32),
            pltpu.VMEM((CELLS, PAD), jnp.int32),
            pltpu.VMEM((SLOTS, 16, PAD), BF16),
            pltpu.VMEM((ROWS * 16, LANES), F32),
            pltpu.VMEM((ROWS, VEC, LANES), F32),
            pltpu.VMEM((ROWS, VEC, LANES), F32),
            pltpu.VMEM((2, 2 * EDGE, VEC, LANES), F32),
            pltpu.VMEM((2, 2 * EDGE, VEC, LANES), F32),
            pltpu.VMEM((2, 8, 128), F32),
            pltpu.VMEM((2, 8, 128), F32),
            pltpu.VMEM((2, OWNED * NPROJ, NPROJ), F32),
            pltpu.VMEM((2, VEC, 128), F32),
            pltpu.VMEM((2, VEC, 128), F32),
            pltpu.VMEM((2, VEC, 128), F32),
            pltpu.VMEM((2, VEC, 128), F32),
            pltpu.VMEM((2, VEC, 128), F32),
            pltpu.VMEM((2, 1, 128), F32),
            pltpu.VMEM((30, 1, 128), F32),
            pltpu.SemaphoreType.DMA((7,)),
            pltpu.SemaphoreType.DMA((SENDS,)),
            pltpu.SemaphoreType.DMA((SENDS,)),
        ],
        compiler_params=pltpu.CompilerParams(
            collective_id=0, has_side_effects=True, vmem_limit_bytes=40 << 20
        ),
    )(
        pltpu.with_memory_space_constraint(cell_count, pltpu.HBM),
        pltpu.with_memory_space_constraint(support_cell, pltpu.HBM),
        pltpu.with_memory_space_constraint(support_atom, pltpu.HBM),
        pltpu.with_memory_space_constraint(support_count, pltpu.HBM),
        pltpu.with_memory_space_constraint(shift, pltpu.HBM),
        pltpu.with_memory_space_constraint(cell_scale, pltpu.HBM),
        pltpu.with_memory_space_constraint(rhs, pltpu.HBM),
        pltpu.with_memory_space_constraint(potential.reshape(52, 128), pltpu.HBM),
        pltpu.with_memory_space_constraint(precond.reshape(52, 128), pltpu.HBM),
        pltpu.with_memory_space_constraint(stiffness, pltpu.HBM),
        pltpu.with_memory_space_constraint(conn, pltpu.HBM),
        pltpu.with_memory_space_constraint(projector.reshape(ENTRIES * NPROJ, ELEM), pltpu.HBM),
        pltpu.with_memory_space_constraint(atom_matrix.reshape(OWNED * NPROJ, NPROJ), pltpu.HBM),
    )

    answer, left = pl.pallas_call(
        hand_over,
        name="hand_over",
        out_shape=(field, field),
        in_specs=[vmem] * 2,
        out_specs=(anywhere, anywhere),
        scratch_shapes=[pltpu.SemaphoreType.DMA((2 * PARTS,))],
    )(
        pltpu.with_memory_space_constraint(answer, pltpu.VMEM),
        pltpu.with_memory_space_constraint(left, pltpu.VMEM),
    )

    def rows(blocks):
        return jnp.transpose(blocks, (1, 0, 2)).reshape(VEC, NODE_DEV)

    return (rows(answer), rows(left))


def solution(mesh):
    in_specs = (
        P(None, "dom"),
        P("dom"),
        P("dom"),
        P(),
        P(),
        P("dom"),
        P("dom", None),
        P(),
        P("dom", None, None),
        P("dom"),
        P("dom"),
        P(),
        P("dom", None, None),
    )
    out_specs = (P(None, "dom"), P(None, "dom"))
    return jax.shard_map(
        on_device, mesh=mesh, in_specs=in_specs, out_specs=out_specs, check_vma=False
    )
```

```python
import jax
import jax.numpy as jnp
from jax import lax
from jax.experimental import pallas as pl
from jax.experimental.pallas import tpu as pltpu
from jax.sharding import PartitionSpec as P

F32 = jnp.float32
BF16 = jnp.bfloat16
HIGH = lax.Precision.HIGHEST
MESH = pl.DeviceIdType.MESH

VEC = 8
NPROJ = 8
ELEM = 343
PAD = 384
CELLS = 32
PAIRS = CELLS // 2
ENTRIES = 8
SLOTS = CELLS + ENTRIES
SLOT_PAIRS = SLOTS // 2
OWNED = 2
NODE_DEV = 6656
GHOST = 416
LANES = 256
OWN = NODE_DEV // LANES
EDGE = 2
ROWS = OWN + 2 * EDGE
SHIFT = EDGE * LANES - GHOST
N_DOM = 256


def kernel(
    count_ref,
    support_cell_ref,
    support_atom_ref,
    support_count_ref,
    shift_ref,
    scale_ref,
    rhs_hbm,
    pot_hbm,
    pre_hbm,
    stiff_hbm,
    conn_hbm,
    proj_hbm,
    atom_hbm,
    sol_ref,
    res_ref,
    rhs_ref,
    pot_ref,
    pre_ref,
    stiff_ref,
    conn_ref,
    proj_ref,
    atom_ref,
    win,
    split_main,
    split_rim,
    onehot,
    pos_ref,
    hi_ref,
    hi_wide,
    values,
    lhs_hi,
    lhs_lo,
    stiff_hi,
    stiff_lo,
    proj_pad,
    spread_ref,
    packed,
    acc,
    v_one,
    v_two,
    rim_left,
    rim_right,
    pre_out,
    pre_in,
    atom_in,
    coef_out,
    coef_m2,
    coef_m1,
    coef_p1,
    coef_p2,
    red_out,
    red_in,
    load_sem,
    send_sem,
    recv_sem,
):
    me = lax.axis_index("dom")

    def ring(step):
        return lax.rem(me + (step + N_DOM), N_DOM)

    low16 = lax.rem(me, 16)
    high16 = lax.div(me, 16)
    stages = (
        [me - low16 + lax.rem(low16 + d, 16) for d in range(1, 16)],
        [low16 + 16 * lax.rem(high16 + d, 16) for d in range(1, 16)],
    )
    greeted = [ring(-2), ring(-1), ring(1), ring(2)]
    for group in stages:
        greeted = greeted + group
    barrier = pltpu.get_barrier_semaphore()
    for other in greeted[0:4]:
        pl.semaphore_signal(barrier, inc=1, device_id=(other,), device_id_type=MESH)

    loads = []
    for i, (src, dst) in enumerate(
        (
            (conn_hbm, conn_ref),
            (rhs_hbm, rhs_ref),
            (pre_hbm, pre_ref),
            (atom_hbm, atom_ref),
            (proj_hbm, proj_ref),
            (stiff_hbm, stiff_ref),
            (pot_hbm, pot_ref),
        )
    ):
        load = pltpu.make_async_copy(src, dst, load_sem.at[i])
        load.start()
        loads.append(load)

    for other in greeted[4:]:
        pl.semaphore_signal(barrier, inc=1, device_id=(other,), device_id_type=MESH)

    used = [0]

    def send(src, dst, target):
        slot = used[0]
        used[0] = slot + 1
        copy = pltpu.make_async_remote_copy(
            src_ref=src,
            dst_ref=dst,
            send_sem=send_sem.at[slot],
            recv_sem=recv_sem.at[slot],
            device_id=(target,),
            device_id_type=MESH,
        )
        copy.start()
        return copy

    class RingCopy:
        def __init__(self, src, dst, step):
            slot = used[0]
            used[0] = slot + 1
            self.copy = pltpu.make_async_remote_copy(
                src_ref=src,
                dst_ref=dst,
                send_sem=send_sem.at[slot],
                recv_sem=recv_sem.at[slot],
                device_id=(ring(step),),
                device_id_type=MESH,
            )
            self.sends = me >= -step if step < 0 else me < N_DOM - step
            self.receives = me < N_DOM + step if step < 0 else me >= step

            @pl.when(self.sends)
            def _():
                self.copy.start()

        def wait(self):
            @pl.when(self.sends)
            def _():
                self.copy.wait_send()

            @pl.when(self.receives)
            def _():
                self.copy.wait_recv()

    def row(ref, index):
        return jnp.broadcast_to(ref[index : index + 1, :], (VEC, 128))

    def wide_row(ref, k):
        return jnp.concatenate([row(ref, 2 * k), row(ref, 2 * k + 1)], axis=1)

    for load in loads[1:4]:
        load.wait()
    dot_acc = jnp.zeros((VEC, 128), F32)
    for k in range(OWN):
        for t in range(2):
            column = LANES * k + 128 * t
            r = rhs_ref[:, column : column + 128]
            p = r * row(pre_ref, 2 * k + t)
            win[EDGE + k, :, 128 * t : 128 * t + 128] = p
            dot_acc = dot_acc + r * p
    gamma = jnp.sum(dot_acc, axis=1, keepdims=True)
    pre_out[...] = jnp.zeros_like(pre_out)
    pre_out[0, 0:4, :] = pre_ref[0:4, :]
    pre_out[1, 0:4, :] = pre_ref[48:52, :]
    pl.semaphore_wait(barrier, len(greeted))
    first = [
        RingCopy(win.at[EDGE : 2 * EDGE], win.at[ROWS - EDGE : ROWS], -1),
        RingCopy(win.at[OWN : OWN + EDGE], win.at[0:EDGE], 1),
        RingCopy(pre_out.at[0], pre_in.at[1], -1),
        RingCopy(pre_out.at[1], pre_in.at[0], 1),
        RingCopy(atom_ref, atom_in.at[1], -1),
        RingCopy(atom_ref, atom_in.at[0], 1),
    ]

    loads[0].wait()
    spread_ref[...] = jnp.full((CELLS, PAD), -1, jnp.int32)
    spread_ref[:, 0:ELEM] = conn_ref[...] + SHIFT
    for c in range(CELLS):
        pos_ref[c] = spread_ref[c : c + 1, :]
    for s in range(ENTRIES):
        pos_ref[CELLS + s] = pos_ref[support_cell_ref[s]]
    number = lax.broadcasted_iota(jnp.int32, (LANES, PAD), 0).astype(jnp.int16)

    def build(c, carry):
        for q in range(2):
            slot = 2 * c + q
            place = pos_ref[slot]
            high = jnp.right_shift(place, 8)
            hi_ref[slot] = high
            hi_wide[slot] = jnp.broadcast_to(high, (16, PAD)).astype(jnp.int16)
            low = jnp.bitwise_and(place, LANES - 1)
            low = jnp.broadcast_to(low, (16, PAD)).astype(jnp.int16)
            one = jnp.ones((16, PAD), BF16)
            zero = jnp.zeros((16, PAD), BF16)
            for r in range(LANES // 16):
                hit = jnp.where(number[16 * r : 16 * r + 16, :] == low, one, zero)
                onehot[c, 16 * r : 16 * r + 16, PAD * q : PAD * q + PAD] = hit
        return carry

    lax.fori_loop(0, SLOT_PAIRS, build, 0)

    live_cells = count_ref[me]

    def split(block):
        up = block.astype(BF16)
        return up, (block - up.astype(F32)).astype(BF16)

    def gather_main(blocks):
        count = len(blocks) * VEC
        for i, k in enumerate(blocks):
            up, down = split(win[k])
            split_main[0, VEC * i : VEC * i + VEC, :] = up
            split_main[1, VEC * i : VEC * i + VEC, :] = down

        def body(c, carry):
            oh = onehot[c]
            g = jnp.dot(split_main[0, 0:count, :], oh, preferred_element_type=F32) + jnp.dot(
                split_main[1, 0:count, :], oh, preferred_element_type=F32
            )
            for q in range(2):
                for t in range(3):
                    h = jnp.broadcast_to(
                        hi_ref[2 * c + q, :, 128 * t : 128 * t + 128], (VEC, 128)
                    )
                    got = jnp.zeros((VEC, 128), F32)
                    at = PAD * q + 128 * t
                    for i, k in enumerate(blocks):
                        got = jnp.where(h == k, g[VEC * i : VEC * i + VEC, at : at + 128], got)
                    values[2 * c + q, :, 128 * t : 128 * t + 128] = got
            return carry

        lax.fori_loop(0, SLOT_PAIRS, body, 0, unroll=10)

    def prepare_rim(blocks):
        count = len(blocks) * VEC
        for i, k in enumerate(blocks):
            up, down = split(win[k])
            split_rim[VEC * i : VEC * i + VEC, :] = up
            split_rim[count + VEC * i : count + VEC * i + VEC, :] = down

    def gather_rim(blocks, first_pair, last_pair, cells):
        count = len(blocks) * VEC

        def body(c, carry):
            g = jnp.dot(split_rim[0 : 2 * count, :], onehot[c], preferred_element_type=F32)
            g = g[0:count] + g[count : 2 * count]
            ups, downs = [], []
            for q in range(2):
                slot = 2 * c + q
                parts = []
                for t in range(3):
                    h = jnp.broadcast_to(hi_ref[slot, :, 128 * t : 128 * t + 128], (VEC, 128))
                    got = values[slot, :, 128 * t : 128 * t + 128]
                    at = PAD * q + 128 * t
                    for i, k in enumerate(blocks):
                        got = jnp.where(h == k, g[VEC * i : VEC * i + VEC, at : at + 128], got)
                    parts.append(got)
                full = jnp.concatenate(parts, axis=1)
                values[slot] = full
                if cells:
                    weight = jnp.where(slot < live_cells, scale_ref[slot], 0.0)
                    up, down = split(full * weight)
                    ups.append(up)
                    downs.append(down)
            if cells:
                lhs_hi[c] = jnp.concatenate(ups, axis=0)
                lhs_lo[c] = jnp.concatenate(downs, axis=0)
            return carry

        lax.fori_loop(first_pair, last_pair, body, 0, unroll=last_pair - first_pair)

    def scatter(first_pair, last_pair):
        def body(c, carry):
            v = jnp.concatenate([packed[2 * c], packed[2 * c + 1]], axis=1)
            h = jnp.concatenate([hi_wide[2 * c], hi_wide[2 * c + 1]], axis=1)
            zero = jnp.zeros_like(v)
            a = jnp.concatenate([jnp.where(h == k, v, zero) for k in range(ROWS)], axis=0)
            acc[...] += lax.dot_general(
                a, onehot[c], (((1,), (1,)), ((), ())), preferred_element_type=F32
            )
            return carry

        lax.fori_loop(first_pair, last_pair, body, 0, unroll=last_pair - first_pair)

    own_blocks = list(range(EDGE, EDGE + OWN))
    ghost_blocks = list(range(EDGE)) + list(range(EDGE + OWN, ROWS))
    inner_blocks = list(range(2 * EDGE, OWN))
    rim_blocks = list(range(2 * EDGE)) + list(range(OWN, ROWS))

    gather_main(own_blocks)

    for load in loads[4:]:
        load.wait()
    stiff_hi[...] = jnp.zeros_like(stiff_hi)
    stiff_lo[...] = jnp.zeros_like(stiff_lo)
    up, down = split(stiff_ref[...])
    stiff_hi[0:ELEM, 0:ELEM] = up
    stiff_lo[0:ELEM, 0:ELEM] = down
    proj_pad[...] = jnp.zeros_like(proj_pad)
    proj_pad[:, 0:ELEM] = proj_ref[...]

    lane64 = lax.broadcasted_iota(jnp.int32, (1, 64), 1)
    entry_of = jnp.right_shift(lane64, 3)
    lane128 = lax.broadcasted_iota(jnp.int32, (1, 128), 1)
    channel_of = jnp.bitwise_and(lane128, 7)
    group_of = jnp.right_shift(lane128, 3)
    live_entries = support_count_ref[me]
    atom_row = jnp.full((1, 64), -1, jnp.int32)
    relative = []
    for s in range(ENTRIES):
        own_atom = jnp.where(s < live_entries, support_atom_ref[s] - (me - 1) * OWNED, -1)
        relative.append(own_atom)
        atom_row = jnp.where(entry_of == s, own_atom, atom_row)
    sublane = lax.broadcasted_iota(jnp.int32, (VEC, 128), 0)
    shift_col = jnp.zeros((VEC, 128), F32)
    for v in range(VEC):
        shift_col = jnp.where(sublane == v, shift_ref[v], shift_col)
    r8 = lax.broadcasted_iota(jnp.int32, (8, 64), 0)
    c64 = lax.broadcasted_iota(jnp.int32, (8, 64), 1)
    tile8 = jnp.where(r8 == jnp.bitwise_and(c64, 7), 1.0, 0.0).astype(F32)
    row_atom = jnp.right_shift(lax.broadcasted_iota(jnp.int32, (48, 64), 0), 3)
    column_atom = jnp.right_shift(lax.broadcasted_iota(jnp.int32, (48, 48), 1), 3)
    for copy in first:
        copy.wait()
    not_first = me > 0
    not_last = me < N_DOM - 1
    for k in range(EDGE):
        win[k] = jnp.where(not_first, win[k], 0.0)
        win[ROWS - EDGE + k] = jnp.where(not_last, win[ROWS - EDGE + k], 0.0)
    atoms_left = jnp.where(not_first, atom_in[0], 0.0)
    atoms_right = jnp.where(not_last, atom_in[1], 0.0)
    atoms = jnp.concatenate([atoms_left, atom_ref[...], atoms_right], axis=0)
    atom_tiled = jnp.dot(atoms, tile8, precision=HIGH, preferred_element_type=F32)
    entry_atoms = jnp.where(row_atom == atom_row, atom_tiled, 0.0)
    owned_column = (column_atom >= OWNED) & (column_atom < 2 * OWNED)
    diagonal_block = (row_atom[:, 0:48] == column_atom) & owned_column
    own_atoms = jnp.where(diagonal_block, atom_tiled[:, 0:48], 0.0)

    def coef_start(step):
        own = jnp.zeros((VEC, 128), F32)
        for s in range(ENTRIES):
            field = values[CELLS + s]
            mine = jnp.zeros((VEC, 128), F32)
            for j in range(NPROJ):
                at = NPROJ * s + j
                sums = jnp.sum(field * proj_pad[at : at + 1, :], axis=1, keepdims=True)
                mine = jnp.where(channel_of == j, sums, mine)
            own = own + jnp.where(group_of == relative[s], mine, 0.0)
        coef_out[step] = own
        copies = [
            RingCopy(coef_out.at[step], coef_p1.at[step], -1),
            RingCopy(coef_out.at[step], coef_m1.at[step], 1),
            RingCopy(coef_out.at[step], coef_p2.at[step], -2),
            RingCopy(coef_out.at[step], coef_m2.at[step], 2),
        ]
        return copies

    def moved(tile, blocks):
        return pltpu.roll(tile, (128 - 16 * blocks) % 128, axis=1)

    def near_sum(step):
        left = jnp.where(not_first, coef_m1[step], 0.0)
        right = jnp.where(not_last, coef_p1[step], 0.0)
        return coef_out[step] + moved(left, 1) + moved(right, -1)

    def coef_finish(step, copies):
        for copy in copies:
            copy.wait()
        left = jnp.where(me > 1, coef_m2[step], 0.0)
        right = jnp.where(me < N_DOM - 2, coef_p2[step], 0.0)
        total = near_sum(step) + moved(left, 2) + moved(right, -2)
        return jnp.dot(total[:, 0:48], entry_atoms, precision=HIGH, preferred_element_type=F32)

    def own_energy(step, copies):
        for copy in copies:
            copy.wait()
        total = near_sum(step)[:, 0:48]
        applied = jnp.dot(total, own_atoms, precision=HIGH, preferred_element_type=F32)
        return jnp.sum(total * applied, axis=1, keepdims=True)

    def support_products(chosen):
        back = jnp.concatenate(
            [jnp.where(entry_of == s, chosen, 0.0) for s in range(ENTRIES)], axis=0
        )
        out = jnp.dot(back, proj_pad[...], precision=HIGH, preferred_element_type=F32)
        for s in range(ENTRIES):
            up, down = split(out[VEC * s : VEC * s + VEC, :])
            packed[CELLS + s] = jnp.concatenate([up, down], axis=0)

    def cell_products():
        uh = lhs_hi[...].reshape(CELLS * VEC, PAD)
        ul = lhs_lo[...].reshape(CELLS * VEC, PAD)
        out = jnp.dot(uh, stiff_hi[...], preferred_element_type=F32)
        out = out + jnp.dot(uh, stiff_lo[...], preferred_element_type=F32)
        out = out + jnp.dot(ul, stiff_hi[...], preferred_element_type=F32)
        energy = jnp.zeros((VEC, PAD), F32)
        for c in range(CELLS):
            full = out[VEC * c : VEC * c + VEC, :]
            up, down = split(full)
            packed[c] = jnp.concatenate([up, down], axis=0)
            energy = energy + full * values[c]
        return energy

    def assembled(k):
        both = acc[16 * k : 16 * k + 8, :] + acc[16 * k + 8 : 16 * k + 16, :]
        if EDGE <= k < EDGE + OWN:
            extra = []
            for t in range(2):
                diagonal = row(pot_ref, 2 * (k - EDGE) + t) + shift_col
                extra.append(diagonal * win[k, :, 128 * t : 128 * t + 128])
            both = both + jnp.concatenate(extra, axis=1)
        return both

    prepare_rim(ghost_blocks)
    gather_rim(ghost_blocks, PAIRS, SLOT_PAIRS, False)
    coefs = coef_start(0)
    gather_rim(ghost_blocks, 0, PAIRS, True)
    cell_products()
    acc[...] = jnp.zeros_like(acc)
    scatter(0, PAIRS)
    term = coef_finish(0, coefs)
    support_products(term)
    scatter(PAIRS, SLOT_PAIRS)
    for k in rim_blocks:
        v_one[k] = assembled(k)
    rims = [
        RingCopy(v_one.at[0 : 2 * EDGE], rim_right.at[0], -1),
        RingCopy(v_one.at[OWN:ROWS], rim_left.at[0], 1),
    ]
    for k in inner_blocks:
        v_one[k] = assembled(k)

    sums = [jnp.zeros((VEC, 128), F32) for _ in range(3)]

    def advance(k, sums):
        a_acc, c_acc, d_acc = sums
        for t in range(2):
            at = slice(128 * t, 128 * t + 128)
            index = 2 * (k - EDGE) + t
            image = v_one[k, :, at]
            a_acc = a_acc + image * win[k, :, at]
            w = image * row(pre_ref, index)
            win[k, :, at] = w
            c_acc = c_acc + image * w
            d_acc = d_acc + (row(pot_ref, index) + shift_col) * w * w
        return [a_acc, c_acc, d_acc]

    for k in inner_blocks:
        sums = advance(k, sums)
    gather_main(inner_blocks)
    for copy in rims:
        copy.wait()
    for k in range(2 * EDGE):
        v_one[k] = v_one[k] + jnp.where(not_first, rim_left[0, k], 0.0)
        v_one[OWN + k] = v_one[OWN + k] + jnp.where(not_last, rim_right[0, k], 0.0)
    for k in rim_blocks:
        if EDGE <= k < EDGE + OWN:
            sums = advance(k, sums)
    for k in range(EDGE):
        for t in range(2):
            at = slice(128 * t, 128 * t + 128)
            left = row(pre_in.at[0], 2 * k + t) * v_one[k, :, at]
            win[k, :, at] = jnp.where(not_first, left, 0.0)
            right = row(pre_in.at[1], 2 * k + t) * v_one[OWN + EDGE + k, :, at]
            win[OWN + EDGE + k, :, at] = jnp.where(not_last, right, 0.0)

    prepare_rim(rim_blocks)
    gather_rim(rim_blocks, PAIRS, SLOT_PAIRS, False)
    coefs = coef_start(1)
    gather_rim(rim_blocks, 0, PAIRS, True)
    energy = cell_products()
    acc[...] = jnp.zeros_like(acc)
    scatter(0, 4)

    a_acc, c_acc, d_acc = sums
    for t in range(3):
        d_acc = d_acc + energy[:, 128 * t : 128 * t + 128]
    column = lax.broadcasted_iota(jnp.int32, (VEC, 128), 1)
    place = column - 4 * sublane
    tile = jnp.zeros((VEC, 128), F32)
    locals_ = (
        gamma,
        jnp.sum(a_acc, axis=1, keepdims=True),
        jnp.sum(c_acc, axis=1, keepdims=True),
        jnp.sum(d_acc, axis=1, keepdims=True),
    )
    for i, value in enumerate(locals_):
        tile = jnp.where(place == i, value, tile)
    tile = tile + jnp.where(place == 3, own_energy(1, coefs[0:2]), 0.0)
    tile = jnp.sum(tile, axis=0, keepdims=True)

    def reduce_start(stage, value):
        red_out[stage] = value
        return [
            send(red_out.at[stage], red_in.at[15 * stage + i], other)
            for i, other in enumerate(stages[stage])
        ]

    def reduce_finish(stage, copies, value):
        for copy in copies:
            copy.wait()
        for i in range(len(copies)):
            value = value + red_in[15 * stage + i]
        return value

    going = reduce_start(0, tile)
    scatter(4, PAIRS)
    term = coef_finish(1, coefs[2:4])
    support_products(term)
    scatter(PAIRS, SLOT_PAIRS)
    for k in rim_blocks:
        v_two[k] = assembled(k)
    rims = [
        RingCopy(v_two.at[0:EDGE], rim_right.at[1, 0:EDGE], -1),
        RingCopy(v_two.at[ROWS - EDGE : ROWS], rim_left.at[1, 0:EDGE], 1),
    ]
    tile = reduce_finish(0, going, tile)
    going = reduce_start(1, tile)
    for k in inner_blocks:
        v_two[k] = assembled(k)
    for copy in rims:
        copy.wait()
    for k in range(EDGE):
        v_two[EDGE + k] = v_two[EDGE + k] + jnp.where(not_first, rim_left[1, k], 0.0)
        v_two[OWN + k] = v_two[OWN + k] + jnp.where(not_last, rim_right[1, k], 0.0)
    tile = reduce_finish(1, going, tile)
    gamma, a_sum, c_sum, d_sum = [
        jnp.sum(jnp.where(place == i, jnp.broadcast_to(tile, (VEC, 128)), 0.0), axis=1, keepdims=True)
        for i in range(4)
    ]
    step_one = gamma / a_sum
    fresh = gamma - 2.0 * step_one * a_sum + step_one * step_one * c_sum
    grow = 1.0 + fresh / gamma
    curve = grow * grow * a_sum - 2.0 * grow * step_one * c_sum + step_one * step_one * d_sum
    step_two = fresh / curve
    along = jnp.broadcast_to(step_one + step_two * grow, (VEC, LANES))
    across = jnp.broadcast_to(step_one * step_two, (VEC, LANES))
    for k in range(OWN):
        r = rhs_ref[:, LANES * k : LANES * k + LANES]
        image = v_one[EDGE + k]
        sol_ref[k] = along * (r * wide_row(pre_ref, k)) - across * win[EDGE + k]
        res_ref[k] = r - along * image + across * v_two[EDGE + k]


PARTS = 2


def hand_over(answer_ref, left_ref, answer_out, left_out, sem):
    copies = []
    size = OWN // PARTS
    for i, (src, dst) in enumerate(((answer_ref, answer_out), (left_ref, left_out))):
        for p in range(PARTS):
            piece = pl.ds(size * p, size)
            copy = pltpu.make_async_copy(src.at[piece], dst.at[piece], sem.at[PARTS * i + p])
            copy.start()
            copies.append(copy)
    for copy in copies:
        copy.wait()


SENDS = 6 + 2 * 4 + 2 * 2 + 30


def on_device(
    rhs,
    potential,
    precond,
    shift,
    stiffness,
    cell_scale,
    conn,
    cell_count,
    projector,
    support_cell,
    support_atom,
    support_count,
    atom_matrix,
):
    vmem = pl.BlockSpec(memory_space=pltpu.VMEM)
    smem = pl.BlockSpec(memory_space=pltpu.SMEM)
    field = jax.ShapeDtypeStruct((OWN, VEC, LANES), F32)
    anywhere = pl.BlockSpec(memory_space=pl.ANY)
    answer, left = pl.pallas_call(
        kernel,
        name="pcg",
        out_shape=(field, field),
        in_specs=[smem] * 6 + [anywhere] * 7,
        out_specs=(vmem, vmem),
        scratch_shapes=[
            pltpu.VMEM((VEC, NODE_DEV), F32),
            pltpu.VMEM((52, 128), F32),
            pltpu.VMEM((52, 128), F32),
            pltpu.VMEM((ELEM, ELEM), F32),
            pltpu.VMEM((CELLS, ELEM), jnp.int32),
            pltpu.VMEM((ENTRIES * NPROJ, ELEM), F32),
            pltpu.VMEM((OWNED * NPROJ, NPROJ), F32),
            pltpu.VMEM((ROWS, VEC, LANES), F32),
            pltpu.VMEM((2, ROWS * VEC, LANES), BF16),
            pltpu.VMEM((4 * EDGE * VEC * 2, LANES), BF16),
            pltpu.VMEM((SLOT_PAIRS, LANES, 2 * PAD), BF16),
            pltpu.VMEM((SLOTS, 1, PAD), jnp.int32),
            pltpu.VMEM((SLOTS, 1, PAD), jnp.int32),
            pltpu.VMEM((SLOTS, 16, PAD), jnp.int16),
            pltpu.VMEM((SLOTS, VEC, PAD), F32),
            pltpu.VMEM((PAIRS, 16, PAD), BF16),
            pltpu.VMEM((PAIRS, 16, PAD), BF16),
            pltpu.VMEM((PAD, PAD), BF16),
            pltpu.VMEM((PAD, PAD), BF16),
            pltpu.VMEM((ENTRIES * NPROJ, PAD), F32),
            pltpu.VMEM((CELLS, PAD), jnp.int32),
            pltpu.VMEM((SLOTS, 16, PAD), BF16),
            pltpu.VMEM((ROWS * 16, LANES), F32),
            pltpu.VMEM((ROWS, VEC, LANES), F32),
            pltpu.VMEM((ROWS, VEC, LANES), F32),
            pltpu.VMEM((2, 2 * EDGE, VEC, LANES), F32),
            pltpu.VMEM((2, 2 * EDGE, VEC, LANES), F32),
            pltpu.VMEM((2, 8, 128), F32),
            pltpu.VMEM((2, 8, 128), F32),
            pltpu.VMEM((2, OWNED * NPROJ, NPROJ), F32),
            pltpu.VMEM((2, VEC, 128), F32),
            pltpu.VMEM((2, VEC, 128), F32),
            pltpu.VMEM((2, VEC, 128), F32),
            pltpu.VMEM((2, VEC, 128), F32),
            pltpu.VMEM((2, VEC, 128), F32),
            pltpu.VMEM((2, 1, 128), F32),
            pltpu.VMEM((30, 1, 128), F32),
            pltpu.SemaphoreType.DMA((7,)),
            pltpu.SemaphoreType.DMA((SENDS,)),
            pltpu.SemaphoreType.DMA((SENDS,)),
        ],
        compiler_params=pltpu.CompilerParams(
            collective_id=0, has_side_effects=True, vmem_limit_bytes=40 << 20
        ),
    )(
        pltpu.with_memory_space_constraint(cell_count, pltpu.HBM),
        pltpu.with_memory_space_constraint(support_cell, pltpu.HBM),
        pltpu.with_memory_space_constraint(support_atom, pltpu.HBM),
        pltpu.with_memory_space_constraint(support_count, pltpu.HBM),
        pltpu.with_memory_space_constraint(shift, pltpu.HBM),
        pltpu.with_memory_space_constraint(cell_scale, pltpu.HBM),
        pltpu.with_memory_space_constraint(rhs, pltpu.HBM),
        pltpu.with_memory_space_constraint(potential.reshape(52, 128), pltpu.HBM),
        pltpu.with_memory_space_constraint(precond.reshape(52, 128), pltpu.HBM),
        pltpu.with_memory_space_constraint(stiffness, pltpu.HBM),
        pltpu.with_memory_space_constraint(conn, pltpu.HBM),
        pltpu.with_memory_space_constraint(projector.reshape(ENTRIES * NPROJ, ELEM), pltpu.HBM),
        pltpu.with_memory_space_constraint(atom_matrix.reshape(OWNED * NPROJ, NPROJ), pltpu.HBM),
    )

    answer, left = pl.pallas_call(
        hand_over,
        name="hand_over",
        out_shape=(field, field),
        in_specs=[vmem] * 2,
        out_specs=(anywhere, anywhere),
        scratch_shapes=[pltpu.SemaphoreType.DMA((2 * PARTS,))],
    )(
        pltpu.with_memory_space_constraint(answer, pltpu.VMEM),
        pltpu.with_memory_space_constraint(left, pltpu.VMEM),
    )

    def rows(blocks):
        return jnp.transpose(blocks, (1, 0, 2)).reshape(VEC, NODE_DEV)

    return (rows(answer), rows(left))


def solution(mesh):
    in_specs = (
        P(None, "dom"),
        P("dom"),
        P("dom"),
        P(),
        P(),
        P("dom"),
        P("dom", None),
        P(),
        P("dom", None, None),
        P("dom"),
        P("dom"),
        P(),
        P("dom", None, None),
    )
    out_specs = (P(None, "dom"), P(None, "dom"))
    return jax.shard_map(
        on_device, mesh=mesh, in_specs=in_specs, out_specs=out_specs, check_vma=False
    )
```
